32 devices in a mesh: groups: 2 (over x), kvp: 16 (over z, y, core).
Axes of the slice: x: 2, y: 2, z: 4, core: 2. Of those that a mesh axis runs over, the one named last changes fastest.
Arguments:
- queries: bfloat16 [512, 4096], P(('groups', 'kvp')), parts along dimension 0, may hold values from -8 to 8
- rotated_span_keys: bfloat16 [512, 512], P(('groups', 'kvp')), parts along dimension 0, may hold values from -8 to 8
- incoming_values: bfloat16 [512, 512], P(('groups', 'kvp')), parts along dimension 0, may hold values from -6 to 6
- stored_keys: bfloat16 [32768, 512], P(('groups', 'kvp')), parts along dimension 0, may hold values from -8 to 8
- stored_values: bfloat16 [32768, 512], P(('groups', 'kvp')), parts along dimension 0, may hold values from -6 to 6
- shard_lens: int32 [32], P('groups'), parts along dimension 0, may hold values from 1 to 1024, 12288 in all
- span_starts: int32 [4], P('groups'), parts along dimension 0, may hold values from 6144 to 12288
Outputs:
- attended: bfloat16 [512, 4096], P(('groups', 'kvp')), parts along dimension 0
The draws below stay inside these ranges and needn't reach their ends.
There are 2 independent parts, one for each index of `groups`. The reference program is written for one: setup_inputs(seed, part) draws one part's arguments, and reference() takes and returns one part's arrays. A program takes and returns all parts, laid end to end along the dimension named above; each array names one. Nothing has to cross between parts.
Inputs may be any that keep to these rules, and one draw needn't show every extreme that they name: `shard_lens`: the lengths of the 16 shards sum to 12288; one shard is full.
All inputs are finite; a program needn't handle non-finite values.
Results may differ from the reference program's by a relative error of at most 0.0023.
Values may be sent and summed in bfloat16 or wider, within the bound.
No kernel may reach another device: no remote copies, remote signals or barrier semaphores. Data moves between devices by JAX's collectives and lax.ppermute only.
A program may use at most 64 MiB of HBM per device.

```python
import math
import jax
import jax.numpy as jnp
import numpy as np
from jax import lax

QUERY_HEADS = 32
KEY_VALUE_HEADS = 4
HEAD_SIZE = 128
SPAN = 128
SPANS = 2
SPAN_TOKENS = 256
DEVICE_SLOTS = 1024
CACHE_SLOTS_ALL = 16384
CACHED = 12288
N_KVP = 16


def draw_queries(key, part):
    vector_width = QUERY_HEADS * HEAD_SIZE
    values = jnp.clip(1.75 * jax.random.normal(jax.random.fold_in(key, 3), (SPAN_TOKENS, vector_width), jnp.float32), -8.0, 8.0)
    return values.astype(jnp.bfloat16)


def draw_stored_keys(key, part):
    vector_width = KEY_VALUE_HEADS * HEAD_SIZE
    values = jnp.clip(1.75 * jax.random.normal(jax.random.fold_in(key, 6), (CACHE_SLOTS_ALL, vector_width), jnp.float32), -8.0, 8.0)
    return values.astype(jnp.bfloat16)


def block_scale(rng, shape, pieces, smallest, top_value):
    level, own = 1.0, jax.random.fold_in(rng, 6)
    for axis_at, shards_of in pieces:
        steps = jnp.exp(jax.random.uniform(jax.random.fold_in(own, axis_at), (shards_of,), jnp.float32, smallest / len(pieces), top_value / len(pieces)))
        level = level * jnp.repeat(steps, shape[axis_at] // shards_of).reshape([-1 if axis == axis_at else 1 for axis in range(len(shape))])
    return level


def profile(count, total, limit, skew):
    weights = [(1 << 20) // math.isqrt(rank ** skew) + 1 for rank in range(2, count + 1)]
    rest, counts = total - limit - (count - 1), [1] * (count - 1)
    while rest > 0:
        free = [i for i in range(count - 1) if counts[i] < limit]
        whole, budget = sum([weights[i] for i in free]), rest
        for i in free:
            extra = min(limit - counts[i], max(1, budget * weights[i] // whole), rest)
            counts[i] = counts[i] + extra
            rest = rest - extra
    return np.array([limit] + counts)


def ragged_sizes(rng, count, total, most, slope):
    if count == 2:
        one = jax.random.randint(rng, (), max(1, total - most), min(most, total - 1) + 1)
        return jnp.stack([one, total - one])
    sizes = jnp.asarray(profile(count, total, most, slope), jnp.int32)
    twos = (count - 1) // 2
    source_of, receiver = sizes[1:1 + 2 * twos:2], sizes[2:2 + 2 * twos:2]
    room = jnp.minimum(source_of - 1, most - receiver)
    shifted = jax.random.randint(jax.random.fold_in(rng, 1), (twos,), 0, 1 << 20) % (room + 1)
    sizes = sizes.at[1:1 + 2 * twos:2].set(source_of - shifted).at[2:2 + 2 * twos:2].set(receiver + shifted)
    return sizes[jax.random.permutation(jax.random.fold_in(rng, 2), count)]


def bell_draw(own_key, dims, width, reach, pieces=(), kind=jnp.bfloat16):
    values = jax.random.normal(own_key, dims, jnp.float32) * width
    if len(pieces) > 0:
        values = block_scale(own_key, dims, pieces, -0.22, 0.18) * values
    return jnp.clip(values, min=-reach, max=reach).astype(kind)


def setup_inputs(seed: int = 0, part: int = 0) -> dict:
    arg_keys = jax.random.split(jax.random.key(seed), 8)
    own_keys = jax.random.split(jax.random.fold_in(arg_keys[7], part), 8)
    queries = draw_queries(jax.random.fold_in(jax.random.fold_in(arg_keys[7], part), 71), part)
    rotated_span_keys = bell_draw(own_keys[1], (SPAN_TOKENS, KEY_VALUE_HEADS * HEAD_SIZE), 2.4, 8.0, ((0, 16),))
    incoming_values = bell_draw(own_keys[2], (SPAN_TOKENS, KEY_VALUE_HEADS * HEAD_SIZE), 1.0, 6.0, ((0, 16),))
    stored_keys = draw_stored_keys(jax.random.fold_in(jax.random.fold_in(arg_keys[7], part), 71), part)
    stored_values = bell_draw(own_keys[4], (CACHE_SLOTS_ALL, KEY_VALUE_HEADS * HEAD_SIZE), 1.0, 6.0, ((0, 16),))
    shard_lens = ragged_sizes(own_keys[5], N_KVP, CACHED, DEVICE_SLOTS, 2).astype(jnp.int32)
    span_starts = jax.random.randint(own_keys[6], (SPANS,), CACHED // 2, CACHED + 1).astype(jnp.int32)
    return {"queries": queries, "rotated_span_keys": rotated_span_keys, "incoming_values": incoming_values, "stored_keys": stored_keys, "stored_values": stored_values, "shard_lens": shard_lens, "span_starts": span_starts}


NEG_LARGE = -1.0e30


def reference(queries, rotated_span_keys, incoming_values, stored_keys, stored_values, shard_lens, span_starts):
    query_group_size = QUERY_HEADS // KEY_VALUE_HEADS
    scale = HEAD_SIZE ** -0.5
    offsets = jnp.cumsum(shard_lens) - shard_lens
    slot_index = jnp.arange(DEVICE_SLOTS, dtype=jnp.int32)
    positions = offsets[:, None] + slot_index[None, :]
    live_slots = slot_index[None, :] < shard_lens[:, None]
    gathered_keys = stored_keys.astype(jnp.float32).reshape(N_KVP, DEVICE_SLOTS, KEY_VALUE_HEADS, HEAD_SIZE)
    gathered_values = stored_values.astype(jnp.float32).reshape(N_KVP, DEVICE_SLOTS, KEY_VALUE_HEADS, HEAD_SIZE)
    span_key_rows = rotated_span_keys.astype(jnp.float32).reshape(SPAN_TOKENS, KEY_VALUE_HEADS, HEAD_SIZE)
    span_value_rows = incoming_values.astype(jnp.float32).reshape(SPAN_TOKENS, KEY_VALUE_HEADS, HEAD_SIZE)
    gathered_query = queries.astype(jnp.float32).reshape(SPAN_TOKENS, KEY_VALUE_HEADS, query_group_size, HEAD_SIZE)
    block_row_range = 4
    key_ids = jnp.arange(SPAN_TOKENS, dtype=jnp.int32)

    def one_block(first):
        row_ids = first + jnp.arange(block_row_range, dtype=jnp.int32)
        rows_here = lax.dynamic_slice_in_dim(gathered_query, first, block_row_range, 0)
        limits = span_starts[row_ids // SPAN]
        visible = live_slots[None] & (positions[None] < limits[:, None, None])
        scores = jnp.einsum("rhgd,skhd->rhgsk", rows_here, gathered_keys) * scale
        visible_mask = visible[:, None, None]
        shard_max = jnp.max(jnp.where(visible_mask, scores, NEG_LARGE), axis=-1)
        weights = jnp.where(visible_mask, jnp.exp(scores - shard_max[..., None]), 0.0)
        shard_total = jnp.sum(weights, axis=-1)
        rounded = lax.optimization_barrier(weights.astype(jnp.bfloat16)).astype(jnp.float32)
        shard_num = jnp.einsum("rhgsk,skhd->rhgsd", rounded, gathered_values)
        span_visible = (key_ids[None, :] // SPAN == row_ids[:, None] // SPAN) & (key_ids[None, :] <= row_ids[:, None])
        span_scores = jnp.einsum("rhgd,jhd->rhgj", rows_here, span_key_rows) * scale
        span_mask = span_visible[:, None, None]
        span_max = jnp.max(jnp.where(span_mask, span_scores, NEG_LARGE), axis=-1)
        span_weights = jnp.where(span_mask, jnp.exp(span_scores - span_max[..., None]), 0.0)
        span_total = jnp.sum(span_weights, axis=-1)
        span_rounded = lax.optimization_barrier(span_weights.astype(jnp.bfloat16)).astype(jnp.float32)
        span_num = jnp.einsum("rhgj,jhd->rhgd", span_rounded, span_value_rows)
        overall = jnp.maximum(jnp.max(shard_max, axis=-1), span_max)
        shard_factor = jnp.exp(shard_max - overall[..., None])
        span_factor = jnp.exp(span_max - overall)
        numerator = jnp.sum(shard_num * shard_factor[..., None], axis=3) + span_num * span_factor[..., None]
        denominator = jnp.sum(shard_total * shard_factor, axis=-1) + span_total * span_factor
        return (numerator / denominator[..., None]).reshape(block_row_range, QUERY_HEADS * HEAD_SIZE).astype(jnp.bfloat16)

    block_starts = jnp.arange(SPAN_TOKENS // block_row_range, dtype=jnp.int32) * block_row_range
    result = lax.map(one_block, block_starts)
    return result.reshape(SPAN_TOKENS, QUERY_HEADS * HEAD_SIZE)
```

```python
import functools

import jax
import jax.numpy as jnp
import numpy as np
from jax import lax
from jax.experimental import pallas as pl
from jax.experimental.pallas import tpu as pltpu
from jax.sharding import PartitionSpec as P

QUERY_HEADS = 32
KEY_VALUE_HEADS = 4
HEAD_SIZE = 128
SPAN = 128
SPANS = 2
GROUP = QUERY_HEADS // KEY_VALUE_HEADS
WIDTH = GROUP * HEAD_SIZE
NEG_LARGE = -1e30
LOG2_SCALE = float(HEAD_SIZE**-0.5 * np.log2(np.e))
CODE = 32767.0
F32, BF16, I16 = jnp.float32, jnp.bfloat16, jnp.int16


def row_limit(meta, shard, span, shards, slots):
    start = jnp.int32(0)
    length = jnp.int32(0)
    for j in range(shards):
        n = meta[1 + j]
        start = start + jnp.where(j < shard, n, 0)
        length = jnp.where(j == shard, n, length)
    limit = meta[1 + shards]
    for j in range(1, SPANS):
        limit = jnp.where(span == j, meta[1 + shards + j], limit)
    return jnp.clip(jnp.minimum(length, limit - start), 0, slots)


def stack_heads(q):
    return jnp.concatenate([q[:, g * HEAD_SIZE : (g + 1) * HEAD_SIZE] for g in range(GROUP)], axis=0)


def attend(q, k, v, bias):
    s = lax.dot_general(q, k, (((1,), (1,)), ((), ())), preferred_element_type=F32) + bias
    m = jnp.max(s, axis=1, keepdims=True)
    w = jnp.exp2((s - m) * LOG2_SCALE)
    t = jnp.sum(w, axis=1, keepdims=True)
    n = jnp.dot(w.astype(BF16), v, preferred_element_type=F32)
    return n, m, t


def merge(a, b):
    if a is None:
        return b
    m = jnp.maximum(a[1], b[1])
    fa, fb = jnp.exp2((a[1] - m) * LOG2_SCALE), jnp.exp2((b[1] - m) * LOG2_SCALE)
    return a[0] * fa + b[0] * fb, m, a[2] * fa + b[2] * fb


def encode(state, out_ref, rows):
    n, m, t = state
    top = jnp.maximum(jnp.max(jnp.abs(n), axis=1, keepdims=True), 1e-30)
    codes = jnp.round(n * (CODE / top)).astype(jnp.int32).astype(I16)
    base = m * LOG2_SCALE
    lane = lax.broadcasted_iota(jnp.int32, (rows, HEAD_SIZE), 1)
    stats = jnp.zeros((rows, HEAD_SIZE), jnp.int32)
    for j, value in enumerate((base + jnp.log2(top), base + jnp.log2(t))):
        value = jnp.maximum(value, -2000.0)
        high = jnp.round(value * 16.0)
        low = jnp.round((value - high * (1 / 16.0)) * 524288.0)
        for i, part in enumerate((high.astype(jnp.int32), low.astype(jnp.int32))):
            for g in range(GROUP):
                stats = jnp.where(lane == 4 * g + 2 * j + i, part[g * rows : (g + 1) * rows], stats)
    for g in range(GROUP):
        out_ref[:, g * HEAD_SIZE : (g + 1) * HEAD_SIZE] = codes[g * rows : (g + 1) * rows]
    out_ref[:, WIDTH:] = stats.astype(I16)


def split_kernel(rows, meta, q_ref, sk_ref, sv_ref, k_ref, v_ref, *outs):
    me = meta[0] % 4
    for j in range(1, 4):
        at = pl.ds(pl.multiple_of((me ^ j) * HEAD_SIZE, HEAD_SIZE), HEAD_SIZE)
        outs[3 + j][:, :HEAD_SIZE] = k_ref[:, at]
        outs[3 + j][:, HEAD_SIZE:] = v_ref[:, at]

    @pl.when(pl.program_id(0) == 0)
    def _():
        for j in range(4):
            at = pl.ds(pl.multiple_of((me ^ j) * HEAD_SIZE, HEAD_SIZE), HEAD_SIZE)
            wide = pl.ds(pl.multiple_of((me ^ j) * WIDTH, WIDTH), WIDTH)
            outs[j][:, :WIDTH] = q_ref[:, wide]
            outs[j][:, WIDTH : WIDTH + HEAD_SIZE] = sk_ref[:, at]
            outs[j][:, WIDTH + HEAD_SIZE :] = sv_ref[:, at]


def whole(shape):
    return pl.BlockSpec(shape, lambda i, meta: (0,) * len(shape))


def split(meta, queries, span_keys, span_values, keys, values):
    rows, slots = queries.shape[0], keys.shape[0]
    steps = 4
    wide = WIDTH + 2 * HEAD_SIZE
    part = slots // steps
    return pl.pallas_call(
        functools.partial(split_kernel, rows),
        out_shape=[jax.ShapeDtypeStruct((rows, wide), BF16)] * 4
        + [jax.ShapeDtypeStruct((slots, 2 * HEAD_SIZE), BF16)] * 3,
        grid_spec=pltpu.PrefetchScalarGridSpec(
            num_scalar_prefetch=1,
            grid=(steps,),
            in_specs=[
                whole(queries.shape),
                whole(span_keys.shape),
                whole(span_values.shape),
                pl.BlockSpec((part, keys.shape[1]), lambda i, meta: (i, 0)),
                pl.BlockSpec((part, keys.shape[1]), lambda i, meta: (i, 0)),
            ],
            out_specs=[whole((rows, wide))] * 4
            + [pl.BlockSpec((part, 2 * HEAD_SIZE), lambda i, meta: (i, 0))] * 3,
        ),
        name="split",
    )(meta, queries, span_keys, span_values, keys, values)


def attend_kernel(cfg, meta, *refs):
    shards, blocks, pieces, own, prior, finish, rows = cfg
    refs = list(refs)
    q_refs = [refs.pop(0) for _ in blocks]
    kv = []
    for j in pieces:
        if own and j == 0:
            kv.append((refs.pop(0), refs.pop(0)))
        else:
            kv.append((refs.pop(0), None))
    prior_refs = [(refs.pop(0), refs.pop(0)) for _ in blocks] if prior else None
    span_ref = refs.pop(0) if finish == "span" else None
    outs = refs
    me = meta[0]
    zs = shards // 4
    z, b = me // 4, me % 4
    slots = kv[0][0].shape[0]
    lane = lax.broadcasted_iota(jnp.int32, (1, slots), 1)
    for i, d in enumerate(blocks):
        q = stack_heads(q_refs[i][:, :WIDTH])
        span = lax.rem(z - d + zs, zs) * rows // SPAN
        state = None
        if prior:
            p_ref, s_ref = prior_refs[i]
            state = (
                jnp.concatenate([p_ref[:, g * HEAD_SIZE : (g + 1) * HEAD_SIZE] for g in range(GROUP)], axis=0),
                s_ref[:, 0:1],
                s_ref[:, 1:2],
            )
        for j, (k_ref, v_ref) in zip(pieces, kv):
            seen = row_limit(meta, z * 4 + (b ^ j), span, shards, slots)
            bias = jnp.where(lane < seen, 0.0, NEG_LARGE)
            if v_ref is None:
                k, v = k_ref[:, :HEAD_SIZE], k_ref[:, HEAD_SIZE:]
            else:
                k, v = k_ref[...], v_ref[...]
            state = merge(state, attend(q, k, v, bias))
        if finish == "encode":
            encode(state, outs[i], rows)
            continue
        if finish == "span":
            mine, before = q_refs[i], span_ref
            k = jnp.concatenate([mine[:, WIDTH : WIDTH + HEAD_SIZE], before[:, WIDTH : WIDTH + HEAD_SIZE]], axis=0)
            v = jnp.concatenate([mine[:, WIDTH + HEAD_SIZE :], before[:, WIDTH + HEAD_SIZE :]], axis=0)
            s = lax.dot_general(q, k, (((1,), (1,)), ((), ())), preferred_element_type=F32)
            part = rows // 4
            r = lax.broadcasted_iota(jnp.int32, s.shape, 0) % rows
            c = lax.broadcasted_iota(jnp.int32, s.shape, 1)
            r = ((r // part) ^ b) * part + r % part
            here = (((c // part) ^ b) * part + c % part <= r) & (c < rows)
            earlier = (c >= rows) & ((z * rows) % SPAN > 0)
            visible = here | earlier
            s = jnp.where(visible, s, NEG_LARGE)
            m = jnp.max(s, axis=1, keepdims=True)
            w = jnp.where(visible, jnp.exp2((s - m) * LOG2_SCALE), 0.0)
            t = jnp.sum(w, axis=1, keepdims=True)
            state = merge(state, (jnp.dot(w.astype(BF16), v, preferred_element_type=F32), m, t))
        n, m, t = state
        for g in range(GROUP):
            outs[2 * i][:, g * HEAD_SIZE : (g + 1) * HEAD_SIZE] = n[g * rows : (g + 1) * rows]
        outs[2 * i + 1][:, 0:1] = m
        outs[2 * i + 1][:, 1:2] = t


def attention(meta, shards, q, pieces, own=None, prior=None, finish=None, before=None, name="attend"):
    blocks = tuple(q)
    rows = q[blocks[0]].shape[0]
    order = ((0,) if own is not None else ()) + tuple(pieces)
    args, specs = [], []

    def add(x, spec=None):
        args.append(x)
        specs.append(spec or whole(x.shape))

    for d in blocks:
        add(q[d])
    if own is not None:
        for x in own:
            add(x, pl.BlockSpec((x.shape[0], HEAD_SIZE), lambda i, meta: (0, meta[0] % 4)))
    for j in pieces:
        add(pieces[j])
    if prior is not None:
        for d in blocks:
            add(prior[d][0])
            add(prior[d][1])
    if finish == "span":
        add(before)
    if finish == "encode":
        shapes = [((rows, WIDTH + HEAD_SIZE), I16)] * len(blocks)
    else:
        shapes = [((rows, WIDTH), F32), ((GROUP * rows, HEAD_SIZE), F32)] * len(blocks)
    slots = args[len(blocks)].shape[0]
    work = len(blocks) * len(order) * GROUP * rows * slots
    outs = pl.pallas_call(
        functools.partial(attend_kernel, (shards, blocks, order, own is not None, prior is not None, finish, rows)),
        out_shape=[jax.ShapeDtypeStruct(s, t) for s, t in shapes],
        grid_spec=pltpu.PrefetchScalarGridSpec(
            num_scalar_prefetch=1,
            grid=(1,),
            in_specs=specs,
            out_specs=[whole(s) for s, _ in shapes],
        ),
        cost_estimate=pl.CostEstimate(
            flops=4 * HEAD_SIZE * work, transcendentals=work, bytes_accessed=sum(x.size * 2 for x in args)
        ),
        name=name,
    )(meta, *args)
    if finish == "encode":
        return dict(zip(blocks, outs))
    return {d: (outs[2 * i], outs[2 * i + 1]) for i, d in enumerate(blocks)}


def final_kernel(rows, n_ref, s_ref, *refs):
    codes, outs = refs[:3], refs[3:]
    part = rows // 4
    stats = [c[:, WIDTH:].astype(F32) for c in codes]
    for g in range(GROUP):
        cols = slice(g * HEAD_SIZE, (g + 1) * HEAD_SIZE)
        head = slice(g * rows, (g + 1) * rows)
        m, t = s_ref[head, 0:1] * LOG2_SCALE, s_ref[head, 1:2]
        tops = [x[:, 4 * g : 4 * g + 1] * (1 / 16.0) + x[:, 4 * g + 1 : 4 * g + 2] * (1 / 524288.0) for x in stats]
        sums = [x[:, 4 * g + 2 : 4 * g + 3] * (1 / 16.0) + x[:, 4 * g + 3 : 4 * g + 4] * (1 / 524288.0) for x in stats]
        over = m
        for x in sums:
            over = jnp.maximum(over, x)
        f = jnp.exp2(m - over)
        n, t = n_ref[:, cols] * f, t * f
        for c, top, total in zip(codes, tops, sums):
            n = n + c[:, cols].astype(F32) * (jnp.exp2(top - over) * (1 / CODE))
            t = t + jnp.exp2(total - over)
        n = (n / t).astype(BF16)
        for k in range(4):
            outs[k][:, cols] = n[k * part : (k + 1) * part]


def final(own, codes):
    rows = own[0].shape[0]
    return pl.pallas_call(
        functools.partial(final_kernel, rows),
        out_shape=[jax.ShapeDtypeStruct((rows // 4, WIDTH), BF16)] * 4,
        name="final",
    )(*own, *codes)


def join_kernel(meta, *refs):
    me = meta[0] % 4
    out = refs[4]
    for j in range(4):
        out[:, pl.ds(pl.multiple_of((me ^ j) * WIDTH, WIDTH), WIDTH)] = refs[j][...]


def join(meta, parts):
    rows = parts[0].shape[0]
    return pl.pallas_call(
        join_kernel,
        out_shape=jax.ShapeDtypeStruct((rows, 4 * WIDTH), BF16),
        grid_spec=pltpu.PrefetchScalarGridSpec(
            num_scalar_prefetch=1,
            grid=(1,),
            in_specs=[whole(p.shape) for p in parts],
            out_specs=whole((rows, 4 * WIDTH)),
        ),
        name="join",
    )(meta, *parts)


def pipelined(queries, span_keys, span_values, keys, values, shard_lens, span_starts):
    n = lax.axis_size("kvp")
    zs = n // 4
    meta = jnp.concatenate([lax.axis_index("kvp").astype(jnp.int32)[None], shard_lens, span_starts])

    def within(x, j):
        return lax.ppermute(x, "kvp", [(i, i ^ j) for i in range(n)])

    def along(x, d):
        return lax.ppermute(x, "kvp", [(i, (i // 4 + d) % zs * 4 + i % 4) for i in range(n)])

    cut = split(meta, queries, span_keys, span_values, keys, values)
    q_parts, kv_parts = cut[:4], cut[4:]
    got = [q_parts[0]] + [within(q_parts[j], j) for j in range(1, 4)]
    own = (keys, values)
    kv = {1: within(kv_parts[0], 1), 2: within(kv_parts[1], 2)}
    last, _ = lax.optimization_barrier((kv_parts[2], kv[2]))
    kv[3] = within(last, 3)
    q = {0: jnp.concatenate(got, axis=0)}
    for d in range(1, zs):
        q[d] = along(q[0], d)

    s0 = attention(meta, n, {0: q[0]}, {1: kv[1]}, own=own, name="attend_a")
    s13 = attention(meta, n, {1: q[1], 3: q[3]}, {1: kv[1], 2: kv[2]}, own=own, name="attend_b")
    s2 = attention(meta, n, {2: q[2]}, {1: kv[1], 2: kv[2]}, own=own, name="attend_c")
    codes = attention(meta, n, {2: q[2]}, {3: kv[3]}, prior=s2, finish="encode", name="attend_d")
    codes |= attention(meta, n, {1: q[1], 3: q[3]}, {3: kv[3]}, prior=s13, finish="encode", name="attend_e")
    back = [along(codes[d], -d) for d in (2, 1, 3)]
    mine = attention(
        meta, n, {0: q[0]}, {2: kv[2], 3: kv[3]}, prior=s0, finish="span", before=q[1], name="attend_f"
    )[0]
    parts = final(mine, back)
    parts = [parts[0]] + [within(parts[j], j) for j in range(1, 4)]
    return join(meta, parts)


def softmax_part(query_rows, per_head_keys, per_head_values, visible, scale):
    scores = (
        jnp.einsum("rhgd,khd->rhgk", query_rows, per_head_keys, preferred_element_type=jnp.float32)
        * scale
    )
    visible_mask = visible[:, None, None, :]
    maxima = jnp.max(jnp.where(visible_mask, scores, NEG_LARGE), axis=-1)
    weights = jnp.where(visible_mask, jnp.exp(scores - maxima[..., None]), 0.0)
    totals = jnp.sum(weights, axis=-1)
    numerators = jnp.einsum(
        "rhgk,khd->rhgd",
        weights.astype(jnp.bfloat16),
        per_head_values,
        preferred_element_type=jnp.float32,
    )
    return (numerators, maxima, totals)


def shards(
    queries, rotated_span_keys, incoming_values, stored_keys, stored_values, shard_lens, span_starts
):
    shard_count = lax.axis_size("kvp")
    device = lax.axis_index("kvp")
    device_local_rows = queries.shape[0]
    cache_slot_count = stored_keys.shape[0]
    query_group_size = QUERY_HEADS // KEY_VALUE_HEADS
    scale = HEAD_SIZE ** (-0.5)
    offsets = jnp.cumsum(shard_lens) - shard_lens
    device_pick = (jnp.arange(shard_count, dtype=jnp.int32) == device).astype(jnp.int32)
    my_start = jnp.sum(offsets * device_pick)
    my_length = jnp.sum(shard_lens * device_pick)
    slot_index = jnp.arange(cache_slot_count, dtype=jnp.int32)
    positions = my_start + slot_index
    live_slots = slot_index < my_length
    per_head_keys = stored_keys.reshape(cache_slot_count, KEY_VALUE_HEADS, HEAD_SIZE)
    per_head_values = stored_values.reshape(cache_slot_count, KEY_VALUE_HEADS, HEAD_SIZE)
    span_index = jnp.arange(SPANS, dtype=jnp.int32)
    every_query = lax.all_gather(queries, "kvp", axis=0, tiled=True)
    overall_rows = every_query.shape[0]
    block_row_range = 64

    def one_block(first):
        rows_here = lax.dynamic_slice_in_dim(every_query, first, block_row_range, 0).reshape(
            block_row_range, KEY_VALUE_HEADS, query_group_size, HEAD_SIZE
        )
        row_ids = first + jnp.arange(block_row_range, dtype=jnp.int32)
        compare = (row_ids // SPAN)[:, None] == span_index[None, :]
        limits = jnp.sum(jnp.where(compare, span_starts[None, :], 0), axis=1)
        visible = live_slots[None, :] & (positions[None, :] < limits[:, None])
        numerators, maxima, totals = softmax_part(
            rows_here, per_head_keys, per_head_values, visible, scale
        )
        return (
            numerators.reshape(block_row_range, QUERY_HEADS * HEAD_SIZE),
            maxima.reshape(block_row_range, QUERY_HEADS),
            totals.reshape(block_row_range, QUERY_HEADS),
        )

    block_starts = jnp.arange(overall_rows // block_row_range, dtype=jnp.int32) * block_row_range
    numerators, maxima, totals = lax.map(one_block, block_starts)
    numerators = numerators.reshape(overall_rows, QUERY_HEADS * HEAD_SIZE)
    maxima = maxima.reshape(overall_rows, QUERY_HEADS)
    totals = totals.reshape(overall_rows, QUERY_HEADS)
    span_key_rows, span_value_rows = (
        lax.all_gather(rotated_span_keys, "kvp", axis=0, tiled=True),
        lax.all_gather(incoming_values, "kvp", axis=0, tiled=True),
    )
    own_ids = device * device_local_rows + jnp.arange(device_local_rows, dtype=jnp.int32)
    key_ids = jnp.arange(overall_rows, dtype=jnp.int32)
    span_visible = (key_ids[None, :] // SPAN == own_ids[:, None] // SPAN) & (
        key_ids[None, :] <= own_ids[:, None]
    )
    local_query = queries.reshape(device_local_rows, KEY_VALUE_HEADS, query_group_size, HEAD_SIZE)
    span_num, span_max, span_total = softmax_part(
        local_query,
        span_key_rows.reshape(overall_rows, KEY_VALUE_HEADS, HEAD_SIZE),
        span_value_rows.reshape(overall_rows, KEY_VALUE_HEADS, HEAD_SIZE),
        span_visible,
        scale,
    )
    span_num = span_num.reshape(device_local_rows, QUERY_HEADS, HEAD_SIZE)
    span_max = span_max.reshape(device_local_rows, QUERY_HEADS)
    span_total = span_total.reshape(device_local_rows, QUERY_HEADS)
    arrived_num, arrived_max, arrived_total = (
        lax.all_to_all(
            numerators.reshape(shard_count, device_local_rows, QUERY_HEADS * HEAD_SIZE),
            "kvp",
            split_axis=0,
            concat_axis=0,
            tiled=True,
        ),
        lax.all_to_all(
            maxima.reshape(shard_count, device_local_rows, QUERY_HEADS),
            "kvp",
            split_axis=0,
            concat_axis=0,
            tiled=True,
        ),
        lax.all_to_all(
            totals.reshape(shard_count, device_local_rows, QUERY_HEADS),
            "kvp",
            split_axis=0,
            concat_axis=0,
            tiled=True,
        ),
    )
    own_max = jnp.max(arrived_max, axis=0)
    factor = jnp.exp(arrived_max - own_max[None])
    summed_num = jnp.sum(
        arrived_num.reshape(shard_count, device_local_rows, QUERY_HEADS, HEAD_SIZE)
        * factor[..., None],
        axis=0,
    )
    summed_total = jnp.sum(arrived_total * factor, axis=0)
    overall = jnp.maximum(own_max, span_max)
    shard_factor = jnp.exp(own_max - overall)
    span_factor = jnp.exp(span_max - overall)
    numerator = summed_num * shard_factor[..., None] + span_num * span_factor[..., None]
    denominator = summed_total * shard_factor + span_total * span_factor
    return (
        (numerator / denominator[..., None])
        .reshape(device_local_rows, QUERY_HEADS * HEAD_SIZE)
        .astype(jnp.bfloat16)
    )


def local(*args):
    queries, keys = args[0], args[3]
    four_by_four = lax.axis_size("kvp") == 16 and queries.shape[0] * 4 * 2 == SPAN and keys.shape[0] % 512 == 0
    return pipelined(*args) if four_by_four else shards(*args)


def solution(mesh):
    in_specs = (
        P(("groups", "kvp"), None),
        P(("groups", "kvp"), None),
        P(("groups", "kvp"), None),
        P(("groups", "kvp"), None),
        P(("groups", "kvp"), None),
        P("groups"),
        P("groups"),
    )
    out_specs = P(("groups", "kvp"), None)
    return jax.shard_map(local, mesh=mesh, in_specs=in_specs, out_specs=out_specs, check_vma=False)
```

```python
import functools

import jax
import jax.numpy as jnp
import numpy as np
from jax import lax
from jax.experimental import pallas as pl
from jax.experimental.pallas import tpu as pltpu
from jax.sharding import PartitionSpec as P

QUERY_HEADS = 32
KEY_VALUE_HEADS = 4
HEAD_SIZE = 128
SPAN = 128
SPANS = 2
GROUP = QUERY_HEADS // KEY_VALUE_HEADS
WIDTH = GROUP * HEAD_SIZE
NEG_LARGE = -1e30
LOG2_SCALE = float(HEAD_SIZE**-0.5 * np.log2(np.e))
CODE = 32767.0
VMEM_GRANT = 24 * 2**20
F32, BF16, I16 = jnp.float32, jnp.bfloat16, jnp.int16


def row_limit(lens, starts, shard, span, shards, slots):
    start = jnp.int32(0)
    length = jnp.int32(0)
    for j in range(shards):
        n = lens[j]
        start = start + jnp.where(j < shard, n, 0)
        length = jnp.where(j == shard, n, length)
    limit = starts[0]
    for j in range(1, SPANS):
        limit = jnp.where(span == j, starts[j], limit)
    return jnp.clip(jnp.minimum(length, limit - start), 0, slots)


def stack_heads(q):
    return jnp.concatenate([q[:, g * HEAD_SIZE : (g + 1) * HEAD_SIZE] for g in range(GROUP)], axis=0)


def attend(q, k, v, bias):
    s = lax.dot_general(q, k, (((1,), (1,)), ((), ())), preferred_element_type=F32) + bias
    m = jnp.max(s, axis=1, keepdims=True)
    w = jnp.exp2((s - m) * LOG2_SCALE)
    t = jnp.sum(w, axis=1, keepdims=True)
    n = jnp.dot(w.astype(BF16), v, preferred_element_type=F32)
    return n, m, t


def merge(a, b):
    if a is None:
        return b
    m = jnp.maximum(a[1], b[1])
    fa, fb = jnp.exp2((a[1] - m) * LOG2_SCALE), jnp.exp2((b[1] - m) * LOG2_SCALE)
    return a[0] * fa + b[0] * fb, m, a[2] * fa + b[2] * fb


def encode(state, out_ref, rows):
    n, m, t = state
    top = jnp.maximum(jnp.max(jnp.abs(n), axis=1, keepdims=True), 1e-30)
    codes = jnp.round(n * (CODE / top)).astype(jnp.int32).astype(I16)
    lane = lax.broadcasted_iota(jnp.int32, (rows, HEAD_SIZE), 1)
    base = jnp.zeros((rows, HEAD_SIZE), F32)
    value = jnp.ones((rows, HEAD_SIZE), F32)
    for g in range(GROUP):
        head = slice(g * rows, (g + 1) * rows)
        out_ref[:, g * HEAD_SIZE : (g + 1) * HEAD_SIZE] = codes[head]
        base = jnp.where(lane % GROUP == g, m[head], base)
        value = jnp.where(lane % GROUP == g, jnp.where(lane < 2 * GROUP, top[head], t[head]), value)
    value = jnp.maximum(base * LOG2_SCALE + jnp.log2(value), -2000.0)
    high = jnp.round(value * 16.0)
    low = jnp.round((value - high * (1 / 16.0)) * 524288.0)
    stats = jnp.where(lane % (2 * GROUP) < GROUP, high, low)
    out_ref[:, WIDTH:] = stats.astype(jnp.int32).astype(I16)


def columns(j, width):
    return pl.ds(pl.multiple_of(((lax.axis_index("kvp") % 4) ^ j) * width, width), width)


def local_call(kernel, shapes, args, tables=(), work=0, scratch=(), space=pltpu.VMEM):
    moved = sum(x.size * x.dtype.itemsize for x in args)
    return pl.pallas_call(
        kernel,
        out_shape=[jax.ShapeDtypeStruct(s, t) for s, t in shapes],
        in_specs=[pl.BlockSpec(memory_space=pltpu.SMEM)] * len(tables)
        + [pl.BlockSpec(memory_space=space)] * len(args),
        out_specs=[pl.BlockSpec(memory_space=pltpu.VMEM)] * len(shapes),
        scratch_shapes=scratch,
        compiler_params=pltpu.CompilerParams(vmem_limit_bytes=VMEM_GRANT),
        cost_estimate=pl.CostEstimate(flops=4 * HEAD_SIZE * work, transcendentals=work, bytes_accessed=moved),
    )(*tables, *args)


def split_kernel(shards, lens, starts, q_ref, sk_ref, sv_ref, k_ref, v_ref, *refs):
    outs, bias_ref, sems = refs[:8], refs[8], refs[9]
    copies = []

    def copy(src, dst):
        copies.append(pltpu.make_async_copy(src, dst, sems.at[len(copies)]))
        copies[-1].start()

    for j in (2, 3, 1, 0):
        at = columns(j, HEAD_SIZE)
        copy(q_ref.at[:, columns(j, WIDTH)], outs[j].at[:, pl.ds(0, WIDTH)])
        copy(sk_ref.at[:, at], outs[j].at[:, pl.ds(WIDTH, HEAD_SIZE)])
        copy(sv_ref.at[:, at], outs[j].at[:, pl.ds(WIDTH + HEAD_SIZE, HEAD_SIZE)])
    for j in (2, 3, 1, 0):
        at = columns(j, HEAD_SIZE)
        copy(k_ref.at[:, at], outs[4 + j].at[:, pl.ds(0, HEAD_SIZE)])
        copy(v_ref.at[:, at], outs[4 + j].at[:, pl.ds(HEAD_SIZE, HEAD_SIZE)])
    me = lax.axis_index("kvp")
    slots = k_ref.shape[0]
    lane = lax.broadcasted_iota(jnp.int32, (1, slots), 1)
    for span in range(SPANS):
        for j in range(4):
            seen = row_limit(lens, starts, me // 4 * 4 + ((me % 4) ^ j), span, shards, slots)
            bias_ref[span * 4 + j : span * 4 + j + 1, :] = jnp.where(lane < seen, 0.0, NEG_LARGE)
    for c in copies:
        c.wait()


def stack_kernel(*refs):
    rows = refs[0].shape[0]
    for j, ref in enumerate(refs[:-1]):
        refs[-1][j * rows : (j + 1) * rows, :] = ref[...]


def attend_kernel(cfg, bias_ref, *refs):
    shards, blocks, pieces, prior, finish, rows = cfg
    refs = list(refs)
    q_refs = [refs.pop(0) for _ in blocks]
    kv = [refs.pop(0) for _ in pieces]
    prior_refs = [(refs.pop(0), refs.pop(0)) for _ in blocks] if prior else None
    span_ref = refs.pop(0) if finish == "span" else None
    outs = refs
    me = lax.axis_index("kvp")
    zs = shards // 4
    z, b = me // 4, me % 4
    for i, d in enumerate(blocks):
        q = stack_heads(q_refs[i][:, :WIDTH])
        span = lax.rem(z - d + zs, zs) * rows // SPAN
        state = None
        if prior:
            p_ref, s_ref = prior_refs[i]
            state = (
                jnp.concatenate([p_ref[:, g * HEAD_SIZE : (g + 1) * HEAD_SIZE] for g in range(GROUP)], axis=0),
                s_ref[:, :HEAD_SIZE],
                s_ref[:, HEAD_SIZE:],
            )
        for j, kv_ref in zip(pieces, kv):
            bias = bias_ref[pl.ds(span * 4 + j, 1), :]
            state = merge(state, attend(q, kv_ref[:, :HEAD_SIZE], kv_ref[:, HEAD_SIZE:], bias))
        if finish == "encode":
            encode(state, outs[i], rows)
            continue
        if finish == "span":
            mine, before = q_refs[i], span_ref
            k = jnp.concatenate([mine[:, WIDTH : WIDTH + HEAD_SIZE], before[:, WIDTH : WIDTH + HEAD_SIZE]], axis=0)
            v = jnp.concatenate([mine[:, WIDTH + HEAD_SIZE :], before[:, WIDTH + HEAD_SIZE :]], axis=0)
            s = lax.dot_general(q, k, (((1,), (1,)), ((), ())), preferred_element_type=F32)
            part = rows // 4
            r = lax.broadcasted_iota(jnp.int32, s.shape, 0) % rows
            c = lax.broadcasted_iota(jnp.int32, s.shape, 1)
            r = ((r // part) ^ b) * part + r % part
            here = (((c // part) ^ b) * part + c % part <= r) & (c < rows)
            earlier = (c >= rows) & ((z * rows) % SPAN > 0)
            visible = here | earlier
            s = jnp.where(visible, s, NEG_LARGE)
            m = jnp.max(s, axis=1, keepdims=True)
            w = jnp.where(visible, jnp.exp2((s - m) * LOG2_SCALE), 0.0)
            t = jnp.sum(w, axis=1, keepdims=True)
            state = merge(state, (jnp.dot(w.astype(BF16), v, preferred_element_type=F32), m, t))
        n, m, t = state
        for g in range(GROUP):
            outs[2 * i][:, g * HEAD_SIZE : (g + 1) * HEAD_SIZE] = n[g * rows : (g + 1) * rows]
        outs[2 * i + 1][:, :HEAD_SIZE] = jnp.broadcast_to(m, n.shape)
        outs[2 * i + 1][:, HEAD_SIZE:] = jnp.broadcast_to(t, n.shape)


def attention(bias, shards, q, pieces, prior=None, finish=None, before=None):
    blocks = tuple(q)
    rows = q[blocks[0]].shape[0]
    args = [bias] + [q[d] for d in blocks] + [pieces[j] for j in pieces]
    if prior is not None:
        args += [x for d in blocks for x in prior[d]]
    if finish == "span":
        args.append(before)
    if finish == "encode":
        shapes = [((rows, WIDTH + HEAD_SIZE), I16)] * len(blocks)
    else:
        shapes = [((rows, WIDTH), F32), ((GROUP * rows, 2 * HEAD_SIZE), F32)] * len(blocks)
    work = len(blocks) * GROUP * rows * sum(x.shape[0] for x in pieces.values())
    cfg = (shards, blocks, tuple(pieces), prior is not None, finish, rows)
    outs = local_call(functools.partial(attend_kernel, cfg), shapes, args, work=work)
    if finish == "encode":
        return dict(zip(blocks, outs))
    return {d: (outs[2 * i], outs[2 * i + 1]) for i, d in enumerate(blocks)}


def final_kernel(rows, n_ref, s_ref, *refs):
    codes, outs = refs[:3], refs[3:]
    part = rows // 4
    lane = lax.broadcasted_iota(jnp.int32, (rows, HEAD_SIZE), 1)
    m = jnp.zeros((rows, HEAD_SIZE), F32)
    t = jnp.zeros((rows, HEAD_SIZE), F32)
    for g in range(GROUP):
        head = slice(g * rows, (g + 1) * rows)
        m = jnp.where(lane == g, s_ref[head, :HEAD_SIZE], m)
        t = jnp.where(lane == g, s_ref[head, HEAD_SIZE:], t)
    m = m * LOG2_SCALE
    tops, sums = [], []
    for c in codes:
        x = c[:, WIDTH:].astype(F32)
        x = x * (1 / 16.0) + pltpu.roll(x, HEAD_SIZE - GROUP, 1) * (1 / 524288.0)
        tops.append(x)
        sums.append(pltpu.roll(x, HEAD_SIZE - 2 * GROUP, 1))
    over = m
    for x in sums:
        over = jnp.maximum(over, x)
    mine = jnp.exp2(m - over)
    total = t * mine
    for x in sums:
        total = total + jnp.exp2(x - over)
    inverse = 1.0 / jnp.where(lane < GROUP, total, 1.0)
    factors = [mine * inverse] + [jnp.exp2(jnp.where(lane < GROUP, x - over, 0.0)) * (inverse * (1 / CODE)) for x in tops]
    for g in range(GROUP):
        cols = slice(g * HEAD_SIZE, (g + 1) * HEAD_SIZE)
        n = n_ref[:, cols] * factors[0][:, g : g + 1]
        for c, f in zip(codes, factors[1:]):
            n = n + c[:, cols].astype(F32) * f[:, g : g + 1]
        n = n.astype(BF16)
        for k in range(4):
            outs[k][:, cols] = n[k * part : (k + 1) * part]


def join_kernel(*refs):
    for j in range(4):
        refs[4][:, columns(j, WIDTH)] = refs[j][...]


def pipelined(queries, span_keys, span_values, keys, values, shard_lens, span_starts):
    n = lax.axis_size("kvp")
    zs = n // 4
    tables = (shard_lens, span_starts)

    def within(x, j):
        return lax.ppermute(x, "kvp", [(i, i ^ j) for i in range(n)])

    def along(x, d):
        return lax.ppermute(x, "kvp", [(i, (i // 4 + d) % zs * 4 + i % 4) for i in range(n)])

    def attend(*args, **kwargs):
        return attention(bias, n, *args, **kwargs)

    part, slots = queries.shape[0], keys.shape[0]
    wide = WIDTH + 2 * HEAD_SIZE
    *cut, bias = local_call(
        functools.partial(split_kernel, n),
        [((part, wide), BF16)] * 4 + [((slots, 2 * HEAD_SIZE), BF16)] * 4 + [((SPANS * 4, slots), F32)],
        (queries, span_keys, span_values, keys, values),
        tables=tables,
        scratch=[pltpu.SemaphoreType.DMA((20,))],
        space=pltpu.HBM,
    )
    q_parts, kv_parts = cut[:4], cut[4:]
    q_parts = [q_parts[0]] + [within(q_parts[j], j) for j in range(1, 4)]
    kv = {0: kv_parts[0]} | {j: within(kv_parts[j], j) for j in (2, 3, 1)}
    q = {0: local_call(stack_kernel, [((4 * part, wide), BF16)], q_parts)[0]}
    for d in range(1, zs):
        q[d] = along(q[0], d)

    near = {j: kv[j] for j in (0, 1)}
    s0 = attend({0: q[0]}, near)
    s13 = attend({1: q[1], 3: q[3]}, near)
    s2 = attend({2: q[2]}, near)
    kv[2], kv[3], s0, s13, s2 = lax.optimization_barrier((kv[2], kv[3], s0, s13, s2))
    far = {j: kv[j] for j in (2, 3)}
    codes = attend({2: q[2]}, far, prior=s2, finish="encode")
    codes |= attend({1: q[1], 3: q[3]}, far, prior=s13, finish="encode")
    back = [along(codes[d], -d) for d in (2, 1, 3)]
    mine = attend({0: q[0]}, far, prior=s0, finish="span", before=q[1])[0]
    parts = local_call(functools.partial(final_kernel, q[0].shape[0]), [((part, WIDTH), BF16)] * 4, (*mine, *back))
    parts = [parts[0]] + [within(parts[j], j) for j in range(1, 4)]
    return local_call(join_kernel, [((part, 4 * WIDTH), BF16)], parts)[0]


def softmax_part(query_rows, per_head_keys, per_head_values, visible, scale):
    scores = (
        jnp.einsum("rhgd,khd->rhgk", query_rows, per_head_keys, preferred_element_type=jnp.float32)
        * scale
    )
    visible_mask = visible[:, None, None, :]
    maxima = jnp.max(jnp.where(visible_mask, scores, NEG_LARGE), axis=-1)
    weights = jnp.where(visible_mask, jnp.exp(scores - maxima[..., None]), 0.0)
    totals = jnp.sum(weights, axis=-1)
    numerators = jnp.einsum(
        "rhgk,khd->rhgd",
        weights.astype(jnp.bfloat16),
        per_head_values,
        preferred_element_type=jnp.float32,
    )
    return (numerators, maxima, totals)


def shards(
    queries, rotated_span_keys, incoming_values, stored_keys, stored_values, shard_lens, span_starts
):
    shard_count = lax.axis_size("kvp")
    device = lax.axis_index("kvp")
    device_local_rows = queries.shape[0]
    cache_slot_count = stored_keys.shape[0]
    query_group_size = QUERY_HEADS // KEY_VALUE_HEADS
    scale = HEAD_SIZE ** (-0.5)
    offsets = jnp.cumsum(shard_lens) - shard_lens
    device_pick = (jnp.arange(shard_count, dtype=jnp.int32) == device).astype(jnp.int32)
    my_start = jnp.sum(offsets * device_pick)
    my_length = jnp.sum(shard_lens * device_pick)
    slot_index = jnp.arange(cache_slot_count, dtype=jnp.int32)
    positions = my_start + slot_index
    live_slots = slot_index < my_length
    per_head_keys = stored_keys.reshape(cache_slot_count, KEY_VALUE_HEADS, HEAD_SIZE)
    per_head_values = stored_values.reshape(cache_slot_count, KEY_VALUE_HEADS, HEAD_SIZE)
    span_index = jnp.arange(SPANS, dtype=jnp.int32)
    every_query = lax.all_gather(queries, "kvp", axis=0, tiled=True)
    overall_rows = every_query.shape[0]
    block_row_range = 64

    def one_block(first):
        rows_here = lax.dynamic_slice_in_dim(every_query, first, block_row_range, 0).reshape(
            block_row_range, KEY_VALUE_HEADS, query_group_size, HEAD_SIZE
        )
        row_ids = first + jnp.arange(block_row_range, dtype=jnp.int32)
        compare = (row_ids // SPAN)[:, None] == span_index[None, :]
        limits = jnp.sum(jnp.where(compare, span_starts[None, :], 0), axis=1)
        visible = live_slots[None, :] & (positions[None, :] < limits[:, None])
        numerators, maxima, totals = softmax_part(
            rows_here, per_head_keys, per_head_values, visible, scale
        )
        return (
            numerators.reshape(block_row_range, QUERY_HEADS * HEAD_SIZE),
            maxima.reshape(block_row_range, QUERY_HEADS),
            totals.reshape(block_row_range, QUERY_HEADS),
        )

    block_starts = jnp.arange(overall_rows // block_row_range, dtype=jnp.int32) * block_row_range
    numerators, maxima, totals = lax.map(one_block, block_starts)
    numerators = numerators.reshape(overall_rows, QUERY_HEADS * HEAD_SIZE)
    maxima = maxima.reshape(overall_rows, QUERY_HEADS)
    totals = totals.reshape(overall_rows, QUERY_HEADS)
    span_key_rows, span_value_rows = (
        lax.all_gather(rotated_span_keys, "kvp", axis=0, tiled=True),
        lax.all_gather(incoming_values, "kvp", axis=0, tiled=True),
    )
    own_ids = device * device_local_rows + jnp.arange(device_local_rows, dtype=jnp.int32)
    key_ids = jnp.arange(overall_rows, dtype=jnp.int32)
    span_visible = (key_ids[None, :] // SPAN == own_ids[:, None] // SPAN) & (
        key_ids[None, :] <= own_ids[:, None]
    )
    local_query = queries.reshape(device_local_rows, KEY_VALUE_HEADS, query_group_size, HEAD_SIZE)
    span_num, span_max, span_total = softmax_part(
        local_query,
        span_key_rows.reshape(overall_rows, KEY_VALUE_HEADS, HEAD_SIZE),
        span_value_rows.reshape(overall_rows, KEY_VALUE_HEADS, HEAD_SIZE),
        span_visible,
        scale,
    )
    span_num = span_num.reshape(device_local_rows, QUERY_HEADS, HEAD_SIZE)
    span_max = span_max.reshape(device_local_rows, QUERY_HEADS)
    span_total = span_total.reshape(device_local_rows, QUERY_HEADS)
    arrived_num, arrived_max, arrived_total = (
        lax.all_to_all(
            numerators.reshape(shard_count, device_local_rows, QUERY_HEADS * HEAD_SIZE),
            "kvp",
            split_axis=0,
            concat_axis=0,
            tiled=True,
        ),
        lax.all_to_all(
            maxima.reshape(shard_count, device_local_rows, QUERY_HEADS),
            "kvp",
            split_axis=0,
            concat_axis=0,
            tiled=True,
        ),
        lax.all_to_all(
            totals.reshape(shard_count, device_local_rows, QUERY_HEADS),
            "kvp",
            split_axis=0,
            concat_axis=0,
            tiled=True,
        ),
    )
    own_max = jnp.max(arrived_max, axis=0)
    factor = jnp.exp(arrived_max - own_max[None])
    summed_num = jnp.sum(
        arrived_num.reshape(shard_count, device_local_rows, QUERY_HEADS, HEAD_SIZE)
        * factor[..., None],
        axis=0,
    )
    summed_total = jnp.sum(arrived_total * factor, axis=0)
    overall = jnp.maximum(own_max, span_max)
    shard_factor = jnp.exp(own_max - overall)
    span_factor = jnp.exp(span_max - overall)
    numerator = summed_num * shard_factor[..., None] + span_num * span_factor[..., None]
    denominator = summed_total * shard_factor + span_total * span_factor
    return (
        (numerator / denominator[..., None])
        .reshape(device_local_rows, QUERY_HEADS * HEAD_SIZE)
        .astype(jnp.bfloat16)
    )


def local(*args):
    queries, keys = args[0], args[3]
    four_by_four = lax.axis_size("kvp") == 16 and queries.shape[0] * 4 * 2 == SPAN and keys.shape[0] % 512 == 0
    if not four_by_four:
        return shards(*args)
    return pipelined(*args)


def solution(mesh):
    in_specs = (
        P(("groups", "kvp"), None),
        P(("groups", "kvp"), None),
        P(("groups", "kvp"), None),
        P(("groups", "kvp"), None),
        P(("groups", "kvp"), None),
        P("groups"),
        P("groups"),
    )
    out_specs = P(("groups", "kvp"), None)
    return jax.shard_map(local, mesh=mesh, in_specs=in_specs, out_specs=out_specs, check_vma=False)
```

```python
import functools

import jax
import jax.numpy as jnp
import numpy as np
from jax import lax
from jax.experimental import pallas as pl
from jax.experimental.pallas import tpu as pltpu
from jax.sharding import PartitionSpec as P

QUERY_HEADS = 32
KEY_VALUE_HEADS = 4
HEAD_SIZE = 128
SPAN = 128
SPANS = 2
GROUP = QUERY_HEADS // KEY_VALUE_HEADS
WIDTH = GROUP * HEAD_SIZE
NEG_LARGE = -1e30
LOG2_SCALE = float(HEAD_SIZE**-0.5 * np.log2(np.e))
CODE = 32767.0
VMEM_GRANT = 24 * 2**20
F32, BF16, I16 = jnp.float32, jnp.bfloat16, jnp.int16


def row_limit(lens, starts, shard, span, shards, slots):
    start = jnp.int32(0)
    length = jnp.int32(0)
    for j in range(shards):
        n = lens[j]
        start = start + jnp.where(j < shard, n, 0)
        length = jnp.where(j == shard, n, length)
    limit = starts[0]
    for j in range(1, SPANS):
        limit = jnp.where(span == j, starts[j], limit)
    return jnp.clip(jnp.minimum(length, limit - start), 0, slots)


def stack_heads(q):
    return jnp.concatenate([q[:, g * HEAD_SIZE : (g + 1) * HEAD_SIZE] for g in range(GROUP)], axis=0)


def attend(q, k, v, bias):
    s = lax.dot_general(q, k, (((1,), (1,)), ((), ())), preferred_element_type=F32) + bias
    m = jnp.max(s, axis=1, keepdims=True)
    w = jnp.exp2((s - m) * LOG2_SCALE)
    t = jnp.sum(w, axis=1, keepdims=True)
    n = jnp.dot(w.astype(BF16), v, preferred_element_type=F32)
    return n, m, t


def merge(a, b):
    if a is None:
        return b
    m = jnp.maximum(a[1], b[1])
    fa, fb = jnp.exp2((a[1] - m) * LOG2_SCALE), jnp.exp2((b[1] - m) * LOG2_SCALE)
    return a[0] * fa + b[0] * fb, m, a[2] * fa + b[2] * fb


def encode(state, out_ref, rows):
    n, m, t = state
    top = jnp.maximum(jnp.max(jnp.abs(n), axis=1, keepdims=True), 1e-30)
    codes = jnp.round(n * (CODE / top)).astype(jnp.int32).astype(I16)
    lane = lax.broadcasted_iota(jnp.int32, (rows, HEAD_SIZE), 1)
    base = jnp.zeros((rows, HEAD_SIZE), F32)
    value = jnp.ones((rows, HEAD_SIZE), F32)
    for g in range(GROUP):
        head = slice(g * rows, (g + 1) * rows)
        out_ref[:, g * HEAD_SIZE : (g + 1) * HEAD_SIZE] = codes[head]
        base = jnp.where(lane % GROUP == g, m[head], base)
        value = jnp.where(lane % GROUP == g, jnp.where(lane < 2 * GROUP, top[head], t[head]), value)
    value = jnp.maximum(base * LOG2_SCALE + jnp.log2(value), -2000.0)
    high = jnp.round(value * 16.0)
    low = jnp.round((value - high * (1 / 16.0)) * 524288.0)
    stats = jnp.where(lane % (2 * GROUP) < GROUP, high, low)
    out_ref[:, WIDTH:] = stats.astype(jnp.int32).astype(I16)


def columns(j, width):
    return pl.ds(pl.multiple_of(((lax.axis_index("kvp") % 4) ^ j) * width, width), width)


def local_call(kernel, shapes, args, work=0, scratch=(), space=pltpu.VMEM):
    moved = sum(x.size * x.dtype.itemsize for x in args)
    return pl.pallas_call(
        kernel,
        out_shape=[jax.ShapeDtypeStruct(s, t) for s, t in shapes],
        in_specs=[pl.BlockSpec(memory_space=space)] * len(args),
        out_specs=[pl.BlockSpec(memory_space=pltpu.VMEM)] * len(shapes),
        scratch_shapes=scratch,
        compiler_params=pltpu.CompilerParams(vmem_limit_bytes=VMEM_GRANT),
        cost_estimate=pl.CostEstimate(flops=4 * HEAD_SIZE * work, transcendentals=work, bytes_accessed=moved),
    )(*args)


def split_kernel(shards, lens_ref, starts_ref, q_ref, sk_ref, sv_ref, k_ref, v_ref, *refs):
    outs, (bias_ref, lens, starts, sems) = refs[:8], refs[8:]
    copies = []

    def copy(src, dst):
        copies.append(pltpu.make_async_copy(src, dst, sems.at[len(copies)]))
        copies[-1].start()

    copy(lens_ref, lens)
    copy(starts_ref, starts)
    for j in (2, 3, 1, 0):
        at = columns(j, HEAD_SIZE)
        copy(q_ref.at[:, columns(j, WIDTH)], outs[j].at[:, pl.ds(0, WIDTH)])
        copy(sk_ref.at[:, at], outs[j].at[:, pl.ds(WIDTH, HEAD_SIZE)])
        copy(sv_ref.at[:, at], outs[j].at[:, pl.ds(WIDTH + HEAD_SIZE, HEAD_SIZE)])
    for j in (2, 3, 1, 0):
        at = columns(j, HEAD_SIZE)
        copy(k_ref.at[:, at], outs[4 + j].at[:, pl.ds(0, HEAD_SIZE)])
        copy(v_ref.at[:, at], outs[4 + j].at[:, pl.ds(HEAD_SIZE, HEAD_SIZE)])
    me = lax.axis_index("kvp")
    slots = k_ref.shape[0]
    for c in copies[:2]:
        c.wait()
    lane = lax.broadcasted_iota(jnp.int32, (1, slots), 1)
    for span in range(SPANS):
        for j in range(4):
            seen = row_limit(lens, starts, me // 4 * 4 + ((me % 4) ^ j), span, shards, slots)
            bias_ref[span * 4 + j : span * 4 + j + 1, :] = jnp.where(lane < seen, 0.0, NEG_LARGE)
    for c in copies[2:]:
        c.wait()


def stack_kernel(*refs):
    rows = refs[0].shape[0]
    for j, ref in enumerate(refs[:-1]):
        refs[-1][j * rows : (j + 1) * rows, :] = ref[...]


def attend_kernel(cfg, bias_ref, *refs):
    _, blocks, pieces, prior, finish, rows = cfg
    refs = list(refs)
    q_refs = [refs.pop(0) for _ in blocks]
    kv = [refs.pop(0) for _ in pieces]
    prior_refs = [(refs.pop(0), refs.pop(0)) for _ in blocks] if prior else None
    span_ref = refs.pop(0) if finish == "span" else None
    outs = refs
    me = lax.axis_index("kvp")
    z, b = me // 4, me % 4
    for i, d in enumerate(blocks):
        q = stack_heads(q_refs[i][:, :WIDTH])
        span = (z ^ d) * rows // SPAN
        state = None
        if prior:
            p_ref, s_ref = prior_refs[i]
            state = (
                jnp.concatenate([p_ref[:, g * HEAD_SIZE : (g + 1) * HEAD_SIZE] for g in range(GROUP)], axis=0),
                s_ref[:, :HEAD_SIZE],
                s_ref[:, HEAD_SIZE:],
            )
        for j, kv_ref in zip(pieces, kv):
            bias = bias_ref[pl.ds(span * 4 + j, 1), :]
            state = merge(state, attend(q, kv_ref[:, :HEAD_SIZE], kv_ref[:, HEAD_SIZE:], bias))
        if finish == "encode":
            encode(state, outs[i], rows)
            continue
        if finish == "span":
            mine, before = q_refs[i], span_ref
            k = jnp.concatenate([mine[:, WIDTH : WIDTH + HEAD_SIZE], before[:, WIDTH : WIDTH + HEAD_SIZE]], axis=0)
            v = jnp.concatenate([mine[:, WIDTH + HEAD_SIZE :], before[:, WIDTH + HEAD_SIZE :]], axis=0)
            s = lax.dot_general(q, k, (((1,), (1,)), ((), ())), preferred_element_type=F32)
            part = rows // 4
            r = lax.broadcasted_iota(jnp.int32, s.shape, 0) % rows
            c = lax.broadcasted_iota(jnp.int32, s.shape, 1)
            r = ((r // part) ^ b) * part + r % part
            here = (((c // part) ^ b) * part + c % part <= r) & (c < rows)
            earlier = (c >= rows) & ((z * rows) % SPAN > 0)
            visible = here | earlier
            s = jnp.where(visible, s, NEG_LARGE)
            m = jnp.max(s, axis=1, keepdims=True)
            w = jnp.where(visible, jnp.exp2((s - m) * LOG2_SCALE), 0.0)
            t = jnp.sum(w, axis=1, keepdims=True)
            state = merge(state, (jnp.dot(w.astype(BF16), v, preferred_element_type=F32), m, t))
        n, m, t = state
        for g in range(GROUP):
            outs[2 * i][:, g * HEAD_SIZE : (g + 1) * HEAD_SIZE] = n[g * rows : (g + 1) * rows]
        outs[2 * i + 1][:, :HEAD_SIZE] = jnp.broadcast_to(m, n.shape)
        outs[2 * i + 1][:, HEAD_SIZE:] = jnp.broadcast_to(t, n.shape)


def attention(bias, shards, q, pieces, prior=None, finish=None, before=None):
    blocks = tuple(q)
    rows = q[blocks[0]].shape[0]
    args = [bias] + [q[d] for d in blocks] + [pieces[j] for j in pieces]
    if prior is not None:
        args += [x for d in blocks for x in prior[d]]
    if finish == "span":
        args.append(before)
    if finish == "encode":
        shapes = [((rows, WIDTH + HEAD_SIZE), I16)] * len(blocks)
    else:
        shapes = [((rows, WIDTH), F32), ((GROUP * rows, 2 * HEAD_SIZE), F32)] * len(blocks)
    work = len(blocks) * GROUP * rows * sum(x.shape[0] for x in pieces.values())
    cfg = (shards, blocks, tuple(pieces), prior is not None, finish, rows)
    outs = local_call(functools.partial(attend_kernel, cfg), shapes, args, work=work)
    if finish == "encode":
        return dict(zip(blocks, outs))
    return {d: (outs[2 * i], outs[2 * i + 1]) for i, d in enumerate(blocks)}


def final_kernel(rows, n_ref, s_ref, *refs):
    codes, outs = refs[:3], refs[3:]
    part = rows // 4
    lane = lax.broadcasted_iota(jnp.int32, (rows, HEAD_SIZE), 1)
    m = jnp.zeros((rows, HEAD_SIZE), F32)
    t = jnp.zeros((rows, HEAD_SIZE), F32)
    for g in range(GROUP):
        head = slice(g * rows, (g + 1) * rows)
        m = jnp.where(lane == g, s_ref[head, :HEAD_SIZE], m)
        t = jnp.where(lane == g, s_ref[head, HEAD_SIZE:], t)
    m = m * LOG2_SCALE
    tops, sums = [], []
    for c in codes:
        x = c[:, WIDTH:].astype(F32)
        x = x * (1 / 16.0) + pltpu.roll(x, HEAD_SIZE - GROUP, 1) * (1 / 524288.0)
        tops.append(x)
        sums.append(pltpu.roll(x, HEAD_SIZE - 2 * GROUP, 1))
    over = m
    for x in sums:
        over = jnp.maximum(over, x)
    mine = jnp.exp2(m - over)
    total = t * mine
    for x in sums:
        total = total + jnp.exp2(x - over)
    inverse = 1.0 / jnp.where(lane < GROUP, total, 1.0)
    factors = [mine * inverse] + [jnp.exp2(jnp.where(lane < GROUP, x - over, 0.0)) * (inverse * (1 / CODE)) for x in tops]
    for g in range(GROUP):
        cols = slice(g * HEAD_SIZE, (g + 1) * HEAD_SIZE)
        n = n_ref[:, cols] * factors[0][:, g : g + 1]
        for c, f in zip(codes, factors[1:]):
            n = n + c[:, cols].astype(F32) * f[:, g : g + 1]
        n = n.astype(BF16)
        for k in range(4):
            outs[k][:, cols] = n[k * part : (k + 1) * part]


def join_kernel(*refs):
    for j in range(4):
        refs[4][:, columns(j, WIDTH)] = refs[j][...]


def pipelined(queries, span_keys, span_values, keys, values, shard_lens, span_starts):
    n = lax.axis_size("kvp")
    zs = n // 4
    tables = (shard_lens, span_starts)

    def within(x, j):
        return lax.ppermute(x, "kvp", [(i, i ^ j) for i in range(n)])

    def along(x, d):
        return lax.ppermute(x, "kvp", [(i, i ^ (4 * d)) for i in range(n)])

    def attend(*args, **kwargs):
        return attention(bias, n, *args, **kwargs)

    part, slots = queries.shape[0], keys.shape[0]
    wide = WIDTH + 2 * HEAD_SIZE
    *cut, bias = local_call(
        functools.partial(split_kernel, n),
        [((part, wide), BF16)] * 4 + [((slots, 2 * HEAD_SIZE), BF16)] * 4 + [((SPANS * 4, slots), F32)],
        [pltpu.with_memory_space_constraint(x, pltpu.HBM) for x in tables + (queries, span_keys, span_values, keys, values)],
        scratch=[pltpu.SMEM(x.shape, x.dtype) for x in tables] + [pltpu.SemaphoreType.DMA((22,))],
        space=pltpu.HBM,
    )
    q_parts, kv_parts = cut[:4], cut[4:]
    q_parts = [q_parts[0]] + [within(q_parts[j], j) for j in range(1, 4)]
    kv = {0: kv_parts[0]} | {j: within(kv_parts[j], j) for j in (2, 3, 1)}
    q = {0: local_call(stack_kernel, [((4 * part, wide), BF16)], q_parts)[0]}
    for d in range(1, zs):
        q[d] = along(q[0], d)

    near = {j: kv[j] for j in (0, 1)}
    s0 = attend({0: q[0]}, near)
    near[2] = kv[2]
    s1 = attend({1: q[1]}, near)
    s23 = attend({2: q[2], 3: q[3]}, near)
    kv[3], s0, s1, s23 = lax.optimization_barrier((kv[3], s0, s1, s23))
    last = {3: kv[3]}
    codes = attend({2: q[2], 3: q[3]}, last, prior=s23, finish="encode")
    codes |= attend({1: q[1]}, last, prior=s1, finish="encode")
    back = [along(codes[d], d) for d in (2, 3, 1)]
    mine = attend({0: q[0]}, {2: kv[2], 3: kv[3]}, prior=s0, finish="span", before=q[1])[0]
    parts = local_call(functools.partial(final_kernel, q[0].shape[0]), [((part, WIDTH), BF16)] * 4, (*mine, *back))
    parts = [parts[0]] + [within(parts[j], j) for j in range(1, 4)]
    return local_call(join_kernel, [((part, 4 * WIDTH), BF16)], parts)[0]


def softmax_part(query_rows, per_head_keys, per_head_values, visible, scale):
    scores = (
        jnp.einsum("rhgd,khd->rhgk", query_rows, per_head_keys, preferred_element_type=jnp.float32)
        * scale
    )
    visible_mask = visible[:, None, None, :]
    maxima = jnp.max(jnp.where(visible_mask, scores, NEG_LARGE), axis=-1)
    weights = jnp.where(visible_mask, jnp.exp(scores - maxima[..., None]), 0.0)
    totals = jnp.sum(weights, axis=-1)
    numerators = jnp.einsum(
        "rhgk,khd->rhgd",
        weights.astype(jnp.bfloat16),
        per_head_values,
        preferred_element_type=jnp.float32,
    )
    return (numerators, maxima, totals)


def shards(
    queries, rotated_span_keys, incoming_values, stored_keys, stored_values, shard_lens, span_starts
):
    shard_count = lax.axis_size("kvp")
    device = lax.axis_index("kvp")
    device_local_rows = queries.shape[0]
    cache_slot_count = stored_keys.shape[0]
    query_group_size = QUERY_HEADS // KEY_VALUE_HEADS
    scale = HEAD_SIZE ** (-0.5)
    offsets = jnp.cumsum(shard_lens) - shard_lens
    device_pick = (jnp.arange(shard_count, dtype=jnp.int32) == device).astype(jnp.int32)
    my_start = jnp.sum(offsets * device_pick)
    my_length = jnp.sum(shard_lens * device_pick)
    slot_index = jnp.arange(cache_slot_count, dtype=jnp.int32)
    positions = my_start + slot_index
    live_slots = slot_index < my_length
    per_head_keys = stored_keys.reshape(cache_slot_count, KEY_VALUE_HEADS, HEAD_SIZE)
    per_head_values = stored_values.reshape(cache_slot_count, KEY_VALUE_HEADS, HEAD_SIZE)
    span_index = jnp.arange(SPANS, dtype=jnp.int32)
    every_query = lax.all_gather(queries, "kvp", axis=0, tiled=True)
    overall_rows = every_query.shape[0]
    block_row_range = 64

    def one_block(first):
        rows_here = lax.dynamic_slice_in_dim(every_query, first, block_row_range, 0).reshape(
            block_row_range, KEY_VALUE_HEADS, query_group_size, HEAD_SIZE
        )
        row_ids = first + jnp.arange(block_row_range, dtype=jnp.int32)
        compare = (row_ids // SPAN)[:, None] == span_index[None, :]
        limits = jnp.sum(jnp.where(compare, span_starts[None, :], 0), axis=1)
        visible = live_slots[None, :] & (positions[None, :] < limits[:, None])
        numerators, maxima, totals = softmax_part(
            rows_here, per_head_keys, per_head_values, visible, scale
        )
        return (
            numerators.reshape(block_row_range, QUERY_HEADS * HEAD_SIZE),
            maxima.reshape(block_row_range, QUERY_HEADS),
            totals.reshape(block_row_range, QUERY_HEADS),
        )

    block_starts = jnp.arange(overall_rows // block_row_range, dtype=jnp.int32) * block_row_range
    numerators, maxima, totals = lax.map(one_block, block_starts)
    numerators = numerators.reshape(overall_rows, QUERY_HEADS * HEAD_SIZE)
    maxima = maxima.reshape(overall_rows, QUERY_HEADS)
    totals = totals.reshape(overall_rows, QUERY_HEADS)
    span_key_rows, span_value_rows = (
        lax.all_gather(rotated_span_keys, "kvp", axis=0, tiled=True),
        lax.all_gather(incoming_values, "kvp", axis=0, tiled=True),
    )
    own_ids = device * device_local_rows + jnp.arange(device_local_rows, dtype=jnp.int32)
    key_ids = jnp.arange(overall_rows, dtype=jnp.int32)
    span_visible = (key_ids[None, :] // SPAN == own_ids[:, None] // SPAN) & (
        key_ids[None, :] <= own_ids[:, None]
    )
    local_query = queries.reshape(device_local_rows, KEY_VALUE_HEADS, query_group_size, HEAD_SIZE)
    span_num, span_max, span_total = softmax_part(
        local_query,
        span_key_rows.reshape(overall_rows, KEY_VALUE_HEADS, HEAD_SIZE),
        span_value_rows.reshape(overall_rows, KEY_VALUE_HEADS, HEAD_SIZE),
        span_visible,
        scale,
    )
    span_num = span_num.reshape(device_local_rows, QUERY_HEADS, HEAD_SIZE)
    span_max = span_max.reshape(device_local_rows, QUERY_HEADS)
    span_total = span_total.reshape(device_local_rows, QUERY_HEADS)
    arrived_num, arrived_max, arrived_total = (
        lax.all_to_all(
            numerators.reshape(shard_count, device_local_rows, QUERY_HEADS * HEAD_SIZE),
            "kvp",
            split_axis=0,
            concat_axis=0,
            tiled=True,
        ),
        lax.all_to_all(
            maxima.reshape(shard_count, device_local_rows, QUERY_HEADS),
            "kvp",
            split_axis=0,
            concat_axis=0,
            tiled=True,
        ),
        lax.all_to_all(
            totals.reshape(shard_count, device_local_rows, QUERY_HEADS),
            "kvp",
            split_axis=0,
            concat_axis=0,
            tiled=True,
        ),
    )
    own_max = jnp.max(arrived_max, axis=0)
    factor = jnp.exp(arrived_max - own_max[None])
    summed_num = jnp.sum(
        arrived_num.reshape(shard_count, device_local_rows, QUERY_HEADS, HEAD_SIZE)
        * factor[..., None],
        axis=0,
    )
    summed_total = jnp.sum(arrived_total * factor, axis=0)
    overall = jnp.maximum(own_max, span_max)
    shard_factor = jnp.exp(own_max - overall)
    span_factor = jnp.exp(span_max - overall)
    numerator = summed_num * shard_factor[..., None] + span_num * span_factor[..., None]
    denominator = summed_total * shard_factor + span_total * span_factor
    return (
        (numerator / denominator[..., None])
        .reshape(device_local_rows, QUERY_HEADS * HEAD_SIZE)
        .astype(jnp.bfloat16)
    )


def local(*args):
    queries, keys = args[0], args[3]
    four_by_four = lax.axis_size("kvp") == 16 and queries.shape[0] * 4 * 2 == SPAN and keys.shape[0] % 512 == 0
    if not four_by_four:
        return shards(*args)
    return pipelined(*args)


def solution(mesh):
    in_specs = (
        P(("groups", "kvp"), None),
        P(("groups", "kvp"), None),
        P(("groups", "kvp"), None),
        P(("groups", "kvp"), None),
        P(("groups", "kvp"), None),
        P("groups"),
        P("groups"),
    )
    out_specs = P(("groups", "kvp"), None)
    return jax.shard_map(local, mesh=mesh, in_specs=in_specs, out_specs=out_specs, check_vma=False)
```

```python
import functools

import jax
import jax.numpy as jnp
import numpy as np
from jax import lax
from jax.experimental import pallas as pl
from jax.experimental.pallas import tpu as pltpu
from jax.sharding import PartitionSpec as P

QUERY_HEADS = 32
KEY_VALUE_HEADS = 4
HEAD_SIZE = 128
SPAN = 128
SPANS = 2
GROUP = QUERY_HEADS // KEY_VALUE_HEADS
WIDTH = GROUP * HEAD_SIZE
NEG_LARGE = -1e30
LOG2_SCALE = float(HEAD_SIZE**-0.5 * np.log2(np.e))
CODE = 32767.0
STATS = 4 * GROUP
VMEM_GRANT = 24 * 2**20
F32, BF16, I16 = jnp.float32, jnp.bfloat16, jnp.int16


def row_limit(lens, starts, shard, span, shards, slots):
    start = jnp.int32(0)
    length = jnp.int32(0)
    for j in range(shards):
        n = lens[j]
        start = start + jnp.where(j < shard, n, 0)
        length = jnp.where(j == shard, n, length)
    limit = starts[0]
    for j in range(1, SPANS):
        limit = jnp.where(span == j, starts[j], limit)
    return jnp.clip(jnp.minimum(length, limit - start), 0, slots)


def stack_heads(q):
    return jnp.concatenate([q[:, g * HEAD_SIZE : (g + 1) * HEAD_SIZE] for g in range(GROUP)], axis=0)


def attend(q, k, v, bias):
    s = lax.dot_general(q, k, (((1,), (1,)), ((), ())), preferred_element_type=F32) + bias
    m = jnp.max(s, axis=1, keepdims=True)
    w = jnp.exp2((s - m) * LOG2_SCALE)
    t = jnp.sum(w, axis=1, keepdims=True)
    n = jnp.dot(w.astype(BF16), v, preferred_element_type=F32)
    return n, m, t


def merge(a, b):
    if a is None:
        return b
    m = jnp.maximum(a[1], b[1])
    fa, fb = jnp.exp2((a[1] - m) * LOG2_SCALE), jnp.exp2((b[1] - m) * LOG2_SCALE)
    return a[0] * fa + b[0] * fb, m, a[2] * fa + b[2] * fb


def encode(state, out_ref, stats_ref, rows):
    n, m, t = state
    top = jnp.maximum(jnp.max(jnp.abs(n), axis=1, keepdims=True), 1e-30)
    codes = jnp.round(n * (CODE / top)).astype(jnp.int32).astype(I16)
    lane = lax.broadcasted_iota(jnp.int32, (rows, HEAD_SIZE), 1)
    base = jnp.zeros((rows, HEAD_SIZE), F32)
    value = jnp.ones((rows, HEAD_SIZE), F32)
    for g in range(GROUP):
        head = slice(g * rows, (g + 1) * rows)
        out_ref[:, g * HEAD_SIZE : (g + 1) * HEAD_SIZE] = codes[head]
        base = jnp.where(lane % GROUP == g, m[head], base)
        value = jnp.where(lane % GROUP == g, jnp.where(lane % STATS < 2 * GROUP, top[head], t[head]), value)
    value = jnp.maximum(base * LOG2_SCALE + jnp.log2(value), -2000.0)
    high = jnp.round(value * 16.0)
    low = jnp.round((value - high * (1 / 16.0)) * 524288.0)
    stats = jnp.where(lane % (2 * GROUP) < GROUP, high, low)
    part = rows // 4
    packed = stats[:part]
    for k in range(1, 4):
        packed = jnp.where(lane[:part] // STATS == k, stats[k * part : (k + 1) * part], packed)
    stats_ref[...] = packed.astype(jnp.int32).astype(I16)


def columns(j, width):
    return pl.ds(pl.multiple_of(((lax.axis_index("kvp") % 4) ^ j) * width, width), width)


def local_call(kernel, shapes, args, work=0, scratch=(), space=pltpu.VMEM):
    moved = sum(x.size * x.dtype.itemsize for x in args)
    return pl.pallas_call(
        kernel,
        out_shape=[jax.ShapeDtypeStruct(s, t) for s, t in shapes],
        in_specs=[pl.BlockSpec(memory_space=space)] * len(args),
        out_specs=[pl.BlockSpec(memory_space=pltpu.VMEM)] * len(shapes),
        scratch_shapes=scratch,
        compiler_params=pltpu.CompilerParams(vmem_limit_bytes=VMEM_GRANT),
        cost_estimate=pl.CostEstimate(flops=4 * HEAD_SIZE * work, transcendentals=work, bytes_accessed=moved),
    )(*args)


def start_all(pairs, sems):
    copies = [pltpu.make_async_copy(src, dst, sems.at[i]) for i, (src, dst) in enumerate(pairs)]
    for c in copies:
        c.start()
    return copies


def split_far_kernel(q_ref, sk_ref, sv_ref, k_ref, v_ref, *refs):
    outs, sems = refs[:6], refs[6]
    pairs = []
    for j in (2, 3, 1, 0):
        at = columns(j, HEAD_SIZE)
        pairs.append((q_ref.at[:, columns(j, WIDTH)], outs[j].at[:, pl.ds(0, WIDTH)]))
        pairs.append((sk_ref.at[:, at], outs[j].at[:, pl.ds(WIDTH, HEAD_SIZE)]))
        pairs.append((sv_ref.at[:, at], outs[j].at[:, pl.ds(WIDTH + HEAD_SIZE, HEAD_SIZE)]))
    for out, j in zip(outs[4:], (2, 3)):
        pairs.append((k_ref.at[:, columns(j, HEAD_SIZE)], out.at[:, pl.ds(0, HEAD_SIZE)]))
        pairs.append((v_ref.at[:, columns(j, HEAD_SIZE)], out.at[:, pl.ds(HEAD_SIZE, HEAD_SIZE)]))
    for c in start_all(pairs, sems):
        c.wait()


def split_near_kernel(shards, lens_ref, starts_ref, k_ref, v_ref, *refs):
    outs, (bias_ref, lens, starts, sems) = refs[:2], refs[2:]
    pairs = [(lens_ref, lens), (starts_ref, starts)]
    for j in (1, 0):
        at = columns(j, HEAD_SIZE)
        pairs.append((k_ref.at[:, at], outs[j].at[:, pl.ds(0, HEAD_SIZE)]))
        pairs.append((v_ref.at[:, at], outs[j].at[:, pl.ds(HEAD_SIZE, HEAD_SIZE)]))
    copies = start_all(pairs, sems)
    me = lax.axis_index("kvp")
    slots = k_ref.shape[0]
    for c in copies[:2]:
        c.wait()
    lane = lax.broadcasted_iota(jnp.int32, (1, slots), 1)
    for span in range(SPANS):
        for j in range(4):
            seen = row_limit(lens, starts, me // 4 * 4 + ((me % 4) ^ j), span, shards, slots)
            bias_ref[span * 4 + j : span * 4 + j + 1, :] = jnp.where(lane < seen, 0.0, NEG_LARGE)
    for c in copies[2:]:
        c.wait()


def stack_kernel(*refs):
    rows = refs[0].shape[0]
    both, only = refs[-2:]
    for j, ref in enumerate(refs[:-2]):
        both[j * rows : (j + 1) * rows, :] = ref[...]
        only[j * rows : (j + 1) * rows, :] = ref[:, :WIDTH]


def attend_kernel(cfg, bias_ref, *refs):
    _, blocks, pieces, prior, finish, rows = cfg
    refs = list(refs)
    q_refs = [refs.pop(0) for _ in blocks]
    kv = [refs.pop(0) for _ in pieces]
    prior_refs = [(refs.pop(0), refs.pop(0)) for _ in blocks] if prior else None
    span_ref = refs.pop(0) if finish == "span" else None
    outs = refs
    me = lax.axis_index("kvp")
    z, b = me // 4, me % 4
    for i, d in enumerate(blocks):
        q = stack_heads(q_refs[i][:, :WIDTH])
        span = (z ^ d) * rows // SPAN
        state = None
        if prior:
            p_ref, s_ref = prior_refs[i]
            state = (
                jnp.concatenate([p_ref[:, g * HEAD_SIZE : (g + 1) * HEAD_SIZE] for g in range(GROUP)], axis=0),
                s_ref[:, :HEAD_SIZE],
                s_ref[:, HEAD_SIZE:],
            )
        for j, kv_ref in zip(pieces, kv):
            bias = bias_ref[pl.ds(span * 4 + j, 1), :]
            state = merge(state, attend(q, kv_ref[:, :HEAD_SIZE], kv_ref[:, HEAD_SIZE:], bias))
        if finish == "encode":
            encode(state, outs[2 * i], outs[2 * i + 1], rows)
            continue
        if finish == "span":
            mine, before = q_refs[i], span_ref
            k = jnp.concatenate([mine[:, WIDTH : WIDTH + HEAD_SIZE], before[:, WIDTH : WIDTH + HEAD_SIZE]], axis=0)
            v = jnp.concatenate([mine[:, WIDTH + HEAD_SIZE :], before[:, WIDTH + HEAD_SIZE :]], axis=0)
            s = lax.dot_general(q, k, (((1,), (1,)), ((), ())), preferred_element_type=F32)
            part = rows // 4
            r = lax.broadcasted_iota(jnp.int32, s.shape, 0) % rows
            c = lax.broadcasted_iota(jnp.int32, s.shape, 1)
            r = ((r // part) ^ b) * part + r % part
            here = (((c // part) ^ b) * part + c % part <= r) & (c < rows)
            earlier = (c >= rows) & ((z * rows) % SPAN > 0)
            visible = here | earlier
            s = jnp.where(visible, s, NEG_LARGE)
            m = jnp.max(s, axis=1, keepdims=True)
            w = jnp.where(visible, jnp.exp2((s - m) * LOG2_SCALE), 0.0)
            t = jnp.sum(w, axis=1, keepdims=True)
            state = merge(state, (jnp.dot(w.astype(BF16), v, preferred_element_type=F32), m, t))
        n, m, t = state
        for g in range(GROUP):
            outs[2 * i][:, g * HEAD_SIZE : (g + 1) * HEAD_SIZE] = n[g * rows : (g + 1) * rows]
        outs[2 * i + 1][:, :HEAD_SIZE] = jnp.broadcast_to(m, n.shape)
        outs[2 * i + 1][:, HEAD_SIZE:] = jnp.broadcast_to(t, n.shape)


def attention(bias, shards, q, pieces, prior=None, finish=None, before=None):
    blocks = tuple(q)
    rows = q[blocks[0]].shape[0]
    args = [bias] + [q[d] for d in blocks] + [pieces[j] for j in pieces]
    if prior is not None:
        args += [x for d in blocks for x in prior[d]]
    if finish == "span":
        args.append(before)
    if finish == "encode":
        shapes = [((rows, WIDTH), I16), ((rows // 4, 4 * STATS), I16)] * len(blocks)
    else:
        shapes = [((rows, WIDTH), F32), ((GROUP * rows, 2 * HEAD_SIZE), F32)] * len(blocks)
    work = len(blocks) * GROUP * rows * sum(x.shape[0] for x in pieces.values())
    cfg = (shards, blocks, tuple(pieces), prior is not None, finish, rows)
    outs = local_call(functools.partial(attend_kernel, cfg), shapes, args, work=work)
    if finish == "encode":
        return outs
    return {d: (outs[2 * i], outs[2 * i + 1]) for i, d in enumerate(blocks)}


def final_kernel(rows, n_ref, s_ref, *refs):
    codes, packed, outs = refs[:6:2], refs[1:6:2], refs[6:]
    part = rows // 4
    lane = lax.broadcasted_iota(jnp.int32, (rows, HEAD_SIZE), 1)
    m = jnp.zeros((rows, HEAD_SIZE), F32)
    t = jnp.zeros((rows, HEAD_SIZE), F32)
    for g in range(GROUP):
        head = slice(g * rows, (g + 1) * rows)
        m = jnp.where(lane == g, s_ref[head, :HEAD_SIZE], m)
        t = jnp.where(lane == g, s_ref[head, HEAD_SIZE:], t)
    m = m * LOG2_SCALE
    tops, sums = [], []
    for p in packed:
        x = p[...].astype(F32)
        x = jnp.concatenate([x] + [pltpu.roll(x, 4 * STATS - k * STATS, 1) for k in range(1, 4)], axis=0)
        x = x * (1 / 16.0) + pltpu.roll(x, HEAD_SIZE - GROUP, 1) * (1 / 524288.0)
        tops.append(x)
        sums.append(pltpu.roll(x, HEAD_SIZE - 2 * GROUP, 1))
    over = m
    for x in sums:
        over = jnp.maximum(over, x)
    mine = jnp.exp2(m - over)
    total = t * mine
    for x in sums:
        total = total + jnp.exp2(x - over)
    inverse = 1.0 / jnp.where(lane < GROUP, total, 1.0)
    factors = [mine * inverse] + [jnp.exp2(jnp.where(lane < GROUP, x - over, 0.0)) * (inverse * (1 / CODE)) for x in tops]
    for g in range(GROUP):
        cols = slice(g * HEAD_SIZE, (g + 1) * HEAD_SIZE)
        n = n_ref[:, cols] * factors[0][:, g : g + 1]
        for c, f in zip(codes, factors[1:]):
            n = n + c[:, cols].astype(F32) * f[:, g : g + 1]
        n = n.astype(BF16)
        for k in range(4):
            outs[k][:, cols] = n[k * part : (k + 1) * part]


def join_kernel(*refs):
    for j in range(4):
        refs[4][:, columns(j, WIDTH)] = refs[j][...]


def pipelined(queries, span_keys, span_values, keys, values, shard_lens, span_starts):
    n = lax.axis_size("kvp")
    zs = n // 4
    tables = (shard_lens, span_starts)

    def within(x, j):
        return lax.ppermute(x, "kvp", [(i, i ^ j) for i in range(n)])

    def along(x, d):
        return lax.ppermute(x, "kvp", [(i, i ^ (4 * d)) for i in range(n)])

    def attend(*args, **kwargs):
        return attention(bias, n, *args, **kwargs)

    part, slots = queries.shape[0], keys.shape[0]
    wide = WIDTH + 2 * HEAD_SIZE
    ins = [queries, span_keys, span_values, keys, values]
    ins, tables = ([pltpu.with_memory_space_constraint(x, pltpu.HBM) for x in xs] for xs in (ins, tables))
    *q_parts, kv2, kv3 = local_call(
        split_far_kernel,
        [((part, wide), BF16)] * 4 + [((slots, 2 * HEAD_SIZE), BF16)] * 2,
        ins,
        scratch=[pltpu.SemaphoreType.DMA((16,))],
        space=pltpu.HBM,
    )
    kv0, kv1, bias = local_call(
        functools.partial(split_near_kernel, n),
        [((slots, 2 * HEAD_SIZE), BF16)] * 2 + [((SPANS * 4, slots), F32)],
        tables + ins[3:],
        scratch=[pltpu.SMEM(x.shape, x.dtype) for x in tables] + [pltpu.SemaphoreType.DMA((6,))],
        space=pltpu.HBM,
    )
    q_parts = [q_parts[0]] + [within(q_parts[j], j) for j in range(1, 4)]
    kv = {0: kv0, 1: within(kv1, 1), 2: within(kv2, 2), 3: within(kv3, 3)}
    both, only = local_call(stack_kernel, [((4 * part, wide), BF16), ((4 * part, WIDTH), BF16)], q_parts)
    q = {0: both, 1: along(both, 1)} | {d: along(only, d) for d in range(2, zs)}

    near = {j: kv[j] for j in (0, 1)}
    state = attend({0: q[0]}, near)
    state |= attend({1: q[1]}, near)
    state = attend({0: q[0], 1: q[1]}, {2: kv[2]}, prior=state)
    near[2] = kv[2]
    state |= attend({2: q[2], 3: q[3]}, near)
    kv[3], state = lax.optimization_barrier((kv[3], state))
    last = {3: kv[3]}
    back = {}
    for d in (2, 3, 1):
        coded, stats = attend({d: q[d]}, last, prior=state, finish="encode")
        back[d] = along(coded, d), along(stats, d)
    back = [x for d in (2, 3, 1) for x in back[d]]
    mine = attend({0: q[0]}, last, prior=state, finish="span", before=q[1])[0]
    parts = local_call(functools.partial(final_kernel, q[0].shape[0]), [((part, WIDTH), BF16)] * 4, (*mine, *back))
    parts = [parts[0]] + [within(parts[j], j) for j in range(1, 4)]
    return local_call(join_kernel, [((part, 4 * WIDTH), BF16)], parts)[0]


def softmax_part(query_rows, per_head_keys, per_head_values, visible, scale):
    scores = (
        jnp.einsum("rhgd,khd->rhgk", query_rows, per_head_keys, preferred_element_type=jnp.float32)
        * scale
    )
    visible_mask = visible[:, None, None, :]
    maxima = jnp.max(jnp.where(visible_mask, scores, NEG_LARGE), axis=-1)
    weights = jnp.where(visible_mask, jnp.exp(scores - maxima[..., None]), 0.0)
    totals = jnp.sum(weights, axis=-1)
    numerators = jnp.einsum(
        "rhgk,khd->rhgd",
        weights.astype(jnp.bfloat16),
        per_head_values,
        preferred_element_type=jnp.float32,
    )
    return (numerators, maxima, totals)


def shards(
    queries, rotated_span_keys, incoming_values, stored_keys, stored_values, shard_lens, span_starts
):
    shard_count = lax.axis_size("kvp")
    device = lax.axis_index("kvp")
    device_local_rows = queries.shape[0]
    cache_slot_count = stored_keys.shape[0]
    query_group_size = QUERY_HEADS // KEY_VALUE_HEADS
    scale = HEAD_SIZE ** (-0.5)
    offsets = jnp.cumsum(shard_lens) - shard_lens
    device_pick = (jnp.arange(shard_count, dtype=jnp.int32) == device).astype(jnp.int32)
    my_start = jnp.sum(offsets * device_pick)
    my_length = jnp.sum(shard_lens * device_pick)
    slot_index = jnp.arange(cache_slot_count, dtype=jnp.int32)
    positions = my_start + slot_index
    live_slots = slot_index < my_length
    per_head_keys = stored_keys.reshape(cache_slot_count, KEY_VALUE_HEADS, HEAD_SIZE)
    per_head_values = stored_values.reshape(cache_slot_count, KEY_VALUE_HEADS, HEAD_SIZE)
    span_index = jnp.arange(SPANS, dtype=jnp.int32)
    every_query = lax.all_gather(queries, "kvp", axis=0, tiled=True)
    overall_rows = every_query.shape[0]
    block_row_range = 64

    def one_block(first):
        rows_here = lax.dynamic_slice_in_dim(every_query, first, block_row_range, 0).reshape(
            block_row_range, KEY_VALUE_HEADS, query_group_size, HEAD_SIZE
        )
        row_ids = first + jnp.arange(block_row_range, dtype=jnp.int32)
        compare = (row_ids // SPAN)[:, None] == span_index[None, :]
        limits = jnp.sum(jnp.where(compare, span_starts[None, :], 0), axis=1)
        visible = live_slots[None, :] & (positions[None, :] < limits[:, None])
        numerators, maxima, totals = softmax_part(
            rows_here, per_head_keys, per_head_values, visible, scale
        )
        return (
            numerators.reshape(block_row_range, QUERY_HEADS * HEAD_SIZE),
            maxima.reshape(block_row_range, QUERY_HEADS),
            totals.reshape(block_row_range, QUERY_HEADS),
        )

    block_starts = jnp.arange(overall_rows // block_row_range, dtype=jnp.int32) * block_row_range
    numerators, maxima, totals = lax.map(one_block, block_starts)
    numerators = numerators.reshape(overall_rows, QUERY_HEADS * HEAD_SIZE)
    maxima = maxima.reshape(overall_rows, QUERY_HEADS)
    totals = totals.reshape(overall_rows, QUERY_HEADS)
    span_key_rows, span_value_rows = (
        lax.all_gather(rotated_span_keys, "kvp", axis=0, tiled=True),
        lax.all_gather(incoming_values, "kvp", axis=0, tiled=True),
    )
    own_ids = device * device_local_rows + jnp.arange(device_local_rows, dtype=jnp.int32)
    key_ids = jnp.arange(overall_rows, dtype=jnp.int32)
    span_visible = (key_ids[None, :] // SPAN == own_ids[:, None] // SPAN) & (
        key_ids[None, :] <= own_ids[:, None]
    )
    local_query = queries.reshape(device_local_rows, KEY_VALUE_HEADS, query_group_size, HEAD_SIZE)
    span_num, span_max, span_total = softmax_part(
        local_query,
        span_key_rows.reshape(overall_rows, KEY_VALUE_HEADS, HEAD_SIZE),
        span_value_rows.reshape(overall_rows, KEY_VALUE_HEADS, HEAD_SIZE),
        span_visible,
        scale,
    )
    span_num = span_num.reshape(device_local_rows, QUERY_HEADS, HEAD_SIZE)
    span_max = span_max.reshape(device_local_rows, QUERY_HEADS)
    span_total = span_total.reshape(device_local_rows, QUERY_HEADS)
    arrived_num, arrived_max, arrived_total = (
        lax.all_to_all(
            numerators.reshape(shard_count, device_local_rows, QUERY_HEADS * HEAD_SIZE),
            "kvp",
            split_axis=0,
            concat_axis=0,
            tiled=True,
        ),
        lax.all_to_all(
            maxima.reshape(shard_count, device_local_rows, QUERY_HEADS),
            "kvp",
            split_axis=0,
            concat_axis=0,
            tiled=True,
        ),
        lax.all_to_all(
            totals.reshape(shard_count, device_local_rows, QUERY_HEADS),
            "kvp",
            split_axis=0,
            concat_axis=0,
            tiled=True,
        ),
    )
    own_max = jnp.max(arrived_max, axis=0)
    factor = jnp.exp(arrived_max - own_max[None])
    summed_num = jnp.sum(
        arrived_num.reshape(shard_count, device_local_rows, QUERY_HEADS, HEAD_SIZE)
        * factor[..., None],
        axis=0,
    )
    summed_total = jnp.sum(arrived_total * factor, axis=0)
    overall = jnp.maximum(own_max, span_max)
    shard_factor = jnp.exp(own_max - overall)
    span_factor = jnp.exp(span_max - overall)
    numerator = summed_num * shard_factor[..., None] + span_num * span_factor[..., None]
    denominator = summed_total * shard_factor + span_total * span_factor
    return (
        (numerator / denominator[..., None])
        .reshape(device_local_rows, QUERY_HEADS * HEAD_SIZE)
        .astype(jnp.bfloat16)
    )


def local(*args):
    queries, keys = args[0], args[3]
    four_by_four = lax.axis_size("kvp") == 16 and queries.shape[0] * 4 * 2 == SPAN and keys.shape[0] % 512 == 0
    if not four_by_four:
        return shards(*args)
    return pipelined(*args)


def solution(mesh):
    in_specs = (
        P(("groups", "kvp"), None),
        P(("groups", "kvp"), None),
        P(("groups", "kvp"), None),
        P(("groups", "kvp"), None),
        P(("groups", "kvp"), None),
        P("groups"),
        P("groups"),
    )
    out_specs = P(("groups", "kvp"), None)
    return jax.shard_map(local, mesh=mesh, in_specs=in_specs, out_specs=out_specs, check_vma=False)
```

```python
import functools

import jax
import jax.numpy as jnp
import numpy as np
from jax import lax
from jax.experimental import pallas as pl
from jax.experimental.pallas import tpu as pltpu
from jax.sharding import PartitionSpec as P

QUERY_HEADS = 32
KEY_VALUE_HEADS = 4
HEAD_SIZE = 128
SPAN = 128
SPANS = 2
GROUP = QUERY_HEADS // KEY_VALUE_HEADS
WIDTH = GROUP * HEAD_SIZE
NEG_LARGE = -1e30
LOG2_SCALE = float(HEAD_SIZE**-0.5 * np.log2(np.e))
CODE = 32767.0
STATS = 4 * GROUP
VMEM_GRANT = 24 * 2**20
F32, BF16, I16 = jnp.float32, jnp.bfloat16, jnp.int16


def row_limit(lens, starts, shard, span, shards, slots):
    start = jnp.int32(0)
    length = jnp.int32(0)
    for j in range(shards):
        n = lens[j]
        start = start + jnp.where(j < shard, n, 0)
        length = jnp.where(j == shard, n, length)
    limit = starts[0]
    for j in range(1, SPANS):
        limit = jnp.where(span == j, starts[j], limit)
    return jnp.clip(jnp.minimum(length, limit - start), 0, slots)


def stack_heads(q):
    return jnp.concatenate([q[:, g * HEAD_SIZE : (g + 1) * HEAD_SIZE] for g in range(GROUP)], axis=0)


def attend(q, k, v, bias):
    s = lax.dot_general(q, k, (((1,), (1,)), ((), ())), preferred_element_type=F32) + bias
    m = jnp.max(s, axis=1, keepdims=True)
    w = jnp.exp2((s - m) * LOG2_SCALE)
    t = jnp.sum(w, axis=1, keepdims=True)
    n = jnp.dot(w.astype(BF16), v, preferred_element_type=F32)
    return n, m, t


def merge(a, b):
    if a is None:
        return b
    m = jnp.maximum(a[1], b[1])
    fa, fb = jnp.exp2((a[1] - m) * LOG2_SCALE), jnp.exp2((b[1] - m) * LOG2_SCALE)
    return a[0] * fa + b[0] * fb, m, a[2] * fa + b[2] * fb


def encode(state, out_ref, rows):
    n, m, t = state
    top = jnp.maximum(jnp.max(jnp.abs(n), axis=1, keepdims=True), 1e-30)
    out_ref[: GROUP * rows, :] = jnp.round(n * (CODE / top)).astype(jnp.int32).astype(I16)
    lane = lax.broadcasted_iota(jnp.int32, (rows, HEAD_SIZE), 1)
    base = jnp.zeros((rows, HEAD_SIZE), F32)
    value = jnp.ones((rows, HEAD_SIZE), F32)
    for g in range(GROUP):
        head = slice(g * rows, (g + 1) * rows)
        base = jnp.where(lane % GROUP == g, m[head], base)
        value = jnp.where(lane % GROUP == g, jnp.where(lane % STATS < 2 * GROUP, top[head], t[head]), value)
    value = jnp.maximum(base * LOG2_SCALE + jnp.log2(value), -2000.0)
    high = jnp.round(value * 16.0)
    low = jnp.round((value - high * (1 / 16.0)) * 524288.0)
    stats = jnp.where(lane % (2 * GROUP) < GROUP, high, low)
    part = rows // 4
    packed = stats[:part]
    for k in range(1, 4):
        packed = jnp.where(lane[:part] // STATS == k, stats[k * part : (k + 1) * part], packed)
    out_ref[GROUP * rows :, :] = packed.astype(jnp.int32).astype(I16)


def columns(j, width):
    return pl.ds(pl.multiple_of(((lax.axis_index("kvp") % 4) ^ j) * width, width), width)


def local_call(kernel, shapes, args, work=0, scratch=(), space=pltpu.VMEM):
    moved = sum(x.size * x.dtype.itemsize for x in args)
    return pl.pallas_call(
        kernel,
        out_shape=[jax.ShapeDtypeStruct(s, t) for s, t in shapes],
        in_specs=[pl.BlockSpec(memory_space=space)] * len(args),
        out_specs=[pl.BlockSpec(memory_space=pltpu.VMEM)] * len(shapes),
        scratch_shapes=scratch,
        compiler_params=pltpu.CompilerParams(vmem_limit_bytes=VMEM_GRANT),
        cost_estimate=pl.CostEstimate(flops=4 * HEAD_SIZE * work, transcendentals=work, bytes_accessed=moved),
    )(*args)


def start_all(pairs, sems):
    copies = [pltpu.make_async_copy(src, dst, sems.at[i]) for i, (src, dst) in enumerate(pairs)]
    for c in copies:
        c.start()
    return copies


def split_far_kernel(q_ref, sk_ref, sv_ref, k_ref, v_ref, *refs):
    outs, sems = refs[:6], refs[6]
    pairs = []
    for j in (2, 3, 1, 0):
        at = columns(j, HEAD_SIZE)
        pairs.append((q_ref.at[:, columns(j, WIDTH)], outs[j].at[:, pl.ds(0, WIDTH)]))
        pairs.append((sk_ref.at[:, at], outs[j].at[:, pl.ds(WIDTH, HEAD_SIZE)]))
        pairs.append((sv_ref.at[:, at], outs[j].at[:, pl.ds(WIDTH + HEAD_SIZE, HEAD_SIZE)]))
    for out, j in zip(outs[4:], (2, 3)):
        pairs.append((k_ref.at[:, columns(j, HEAD_SIZE)], out.at[:, pl.ds(0, HEAD_SIZE)]))
        pairs.append((v_ref.at[:, columns(j, HEAD_SIZE)], out.at[:, pl.ds(HEAD_SIZE, HEAD_SIZE)]))
    for c in start_all(pairs, sems):
        c.wait()


def split_near_kernel(shards, lens_ref, starts_ref, k_ref, v_ref, *refs):
    outs, (bias_ref, lens, starts, sems) = refs[:2], refs[2:]
    pairs = [(lens_ref, lens), (starts_ref, starts)]
    for j in (1, 0):
        at = columns(j, HEAD_SIZE)
        pairs.append((k_ref.at[:, at], outs[j].at[:, pl.ds(0, HEAD_SIZE)]))
        pairs.append((v_ref.at[:, at], outs[j].at[:, pl.ds(HEAD_SIZE, HEAD_SIZE)]))
    copies = start_all(pairs, sems)
    me = lax.axis_index("kvp")
    slots = k_ref.shape[0]
    for c in copies[:2]:
        c.wait()
    lane = lax.broadcasted_iota(jnp.int32, (1, slots), 1)
    for span in range(SPANS):
        for j in range(4):
            seen = row_limit(lens, starts, me // 4 * 4 + ((me % 4) ^ j), span, shards, slots)
            bias_ref[span * 4 + j : span * 4 + j + 1, :] = jnp.where(lane < seen, 0.0, NEG_LARGE)
    for c in copies[2:]:
        c.wait()


def stack_kernel(*refs):
    rows = refs[0].shape[0]
    both, only = refs[-2:]
    for j, ref in enumerate(refs[:-2]):
        both[j * rows : (j + 1) * rows, :] = ref[...]
        only[j * rows : (j + 1) * rows, :] = ref[:, :WIDTH]


def attend_kernel(cfg, bias_ref, *refs):
    _, blocks, pieces, prior, finish, rows = cfg
    refs = list(refs)
    q_refs = [refs.pop(0) for _ in blocks]
    kv = [refs.pop(0) for _ in pieces]
    prior_refs = [(refs.pop(0), refs.pop(0)) for _ in blocks] if prior else None
    span_ref = refs.pop(0) if finish == "span" else None
    outs = refs
    me = lax.axis_index("kvp")
    z, b = me // 4, me % 4
    for i, d in enumerate(blocks):
        q = stack_heads(q_refs[i][:, :WIDTH])
        span = (z ^ d) * rows // SPAN
        state = None
        if prior:
            p_ref, s_ref = prior_refs[i]
            state = (
                jnp.concatenate([p_ref[:, g * HEAD_SIZE : (g + 1) * HEAD_SIZE] for g in range(GROUP)], axis=0),
                s_ref[:, :HEAD_SIZE],
                s_ref[:, HEAD_SIZE:],
            )
        for j, kv_ref in zip(pieces, kv):
            bias = bias_ref[pl.ds(span * 4 + j, 1), :]
            state = merge(state, attend(q, kv_ref[:, :HEAD_SIZE], kv_ref[:, HEAD_SIZE:], bias))
        if finish == "encode":
            encode(state, outs[i], rows)
            continue
        if finish == "span":
            mine, before = q_refs[i], span_ref
            k = jnp.concatenate([mine[:, WIDTH : WIDTH + HEAD_SIZE], before[:, WIDTH : WIDTH + HEAD_SIZE]], axis=0)
            v = jnp.concatenate([mine[:, WIDTH + HEAD_SIZE :], before[:, WIDTH + HEAD_SIZE :]], axis=0)
            s = lax.dot_general(q, k, (((1,), (1,)), ((), ())), preferred_element_type=F32)
            part = rows // 4
            r = lax.broadcasted_iota(jnp.int32, s.shape, 0) % rows
            c = lax.broadcasted_iota(jnp.int32, s.shape, 1)
            r = ((r // part) ^ b) * part + r % part
            here = (((c // part) ^ b) * part + c % part <= r) & (c < rows)
            earlier = (c >= rows) & ((z * rows) % SPAN > 0)
            visible = here | earlier
            s = jnp.where(visible, s, NEG_LARGE)
            m = jnp.max(s, axis=1, keepdims=True)
            w = jnp.where(visible, jnp.exp2((s - m) * LOG2_SCALE), 0.0)
            t = jnp.sum(w, axis=1, keepdims=True)
            state = merge(state, (jnp.dot(w.astype(BF16), v, preferred_element_type=F32), m, t))
        n, m, t = state
        for g in range(GROUP):
            outs[2 * i][:, g * HEAD_SIZE : (g + 1) * HEAD_SIZE] = n[g * rows : (g + 1) * rows]
        outs[2 * i + 1][:, :HEAD_SIZE] = jnp.broadcast_to(m, n.shape)
        outs[2 * i + 1][:, HEAD_SIZE:] = jnp.broadcast_to(t, n.shape)


def attention(bias, shards, q, pieces, prior=None, finish=None, before=None):
    blocks = tuple(q)
    rows = q[blocks[0]].shape[0]
    args = [bias] + [q[d] for d in blocks] + [pieces[j] for j in pieces]
    if prior is not None:
        args += [x for d in blocks for x in prior[d]]
    if finish == "span":
        args.append(before)
    if finish == "encode":
        shapes = [((GROUP * rows + rows // 4, HEAD_SIZE), I16)] * len(blocks)
    else:
        shapes = [((rows, WIDTH), F32), ((GROUP * rows, 2 * HEAD_SIZE), F32)] * len(blocks)
    work = len(blocks) * GROUP * rows * sum(x.shape[0] for x in pieces.values())
    cfg = (shards, blocks, tuple(pieces), prior is not None, finish, rows)
    outs = local_call(functools.partial(attend_kernel, cfg), shapes, args, work=work)
    if finish == "encode":
        return outs
    return {d: (outs[2 * i], outs[2 * i + 1]) for i, d in enumerate(blocks)}


def final_kernel(rows, n_ref, s_ref, *refs):
    codes, outs = refs[:3], refs[3:]
    part = rows // 4
    lane = lax.broadcasted_iota(jnp.int32, (rows, HEAD_SIZE), 1)
    m = jnp.zeros((rows, HEAD_SIZE), F32)
    t = jnp.zeros((rows, HEAD_SIZE), F32)
    for g in range(GROUP):
        head = slice(g * rows, (g + 1) * rows)
        m = jnp.where(lane == g, s_ref[head, :HEAD_SIZE], m)
        t = jnp.where(lane == g, s_ref[head, HEAD_SIZE:], t)
    m = m * LOG2_SCALE
    tops, sums = [], []
    for c in codes:
        x = c[GROUP * rows :, :].astype(F32)
        x = jnp.concatenate([x] + [pltpu.roll(x, 4 * STATS - k * STATS, 1) for k in range(1, 4)], axis=0)
        x = x * (1 / 16.0) + pltpu.roll(x, HEAD_SIZE - GROUP, 1) * (1 / 524288.0)
        tops.append(x)
        sums.append(pltpu.roll(x, HEAD_SIZE - 2 * GROUP, 1))
    over = m
    for x in sums:
        over = jnp.maximum(over, x)
    mine = jnp.exp2(m - over)
    total = t * mine
    for x in sums:
        total = total + jnp.exp2(x - over)
    inverse = 1.0 / jnp.where(lane < GROUP, total, 1.0)
    factors = [mine * inverse] + [jnp.exp2(jnp.where(lane < GROUP, x - over, 0.0)) * (inverse * (1 / CODE)) for x in tops]
    for g in range(GROUP):
        cols = slice(g * HEAD_SIZE, (g + 1) * HEAD_SIZE)
        n = n_ref[:, cols] * factors[0][:, g : g + 1]
        for c, f in zip(codes, factors[1:]):
            n = n + c[g * rows : (g + 1) * rows, :].astype(F32) * f[:, g : g + 1]
        n = n.astype(BF16)
        for k in range(4):
            outs[k][:, cols] = n[k * part : (k + 1) * part]


def join_kernel(*refs):
    for j in range(4):
        refs[4][:, columns(j, WIDTH)] = refs[j][...]


def pipelined(queries, span_keys, span_values, keys, values, shard_lens, span_starts):
    n = lax.axis_size("kvp")
    zs = n // 4
    tables = (shard_lens, span_starts)

    def within(x, j):
        return lax.ppermute(x, "kvp", [(i, i ^ j) for i in range(n)])

    def along(x, d):
        return lax.ppermute(x, "kvp", [(i, i ^ (4 * d)) for i in range(n)])

    def attend(*args, **kwargs):
        return attention(bias, n, *args, **kwargs)

    part, slots = queries.shape[0], keys.shape[0]
    wide = WIDTH + 2 * HEAD_SIZE
    ins = [queries, span_keys, span_values, keys, values]
    ins, tables = ([pltpu.with_memory_space_constraint(x, pltpu.HBM) for x in xs] for xs in (ins, tables))
    *q_parts, kv2, kv3 = local_call(
        split_far_kernel,
        [((part, wide), BF16)] * 4 + [((slots, 2 * HEAD_SIZE), BF16)] * 2,
        ins,
        scratch=[pltpu.SemaphoreType.DMA((16,))],
        space=pltpu.HBM,
    )
    kv0, kv1, bias = local_call(
        functools.partial(split_near_kernel, n),
        [((slots, 2 * HEAD_SIZE), BF16)] * 2 + [((SPANS * 4, slots), F32)],
        tables + ins[3:],
        scratch=[pltpu.SMEM(x.shape, x.dtype) for x in tables] + [pltpu.SemaphoreType.DMA((6,))],
        space=pltpu.HBM,
    )
    q_parts = [q_parts[0]] + [within(q_parts[j], j) for j in range(1, 4)]
    kv = {0: kv0, 1: within(kv1, 1), 2: within(kv2, 2), 3: within(kv3, 3)}
    both, only = local_call(stack_kernel, [((4 * part, wide), BF16), ((4 * part, WIDTH), BF16)], q_parts)
    q = {0: both, 1: along(both, 1)} | {d: along(only, d) for d in range(2, zs)}

    near = {j: kv[j] for j in (0, 1)}
    state = attend({0: q[0]}, near)
    state |= attend({1: q[1]}, near)
    state = attend({0: q[0], 1: q[1]}, {2: kv[2]}, prior=state)
    near[2] = kv[2]
    state |= attend({2: q[2], 3: q[3]}, near)
    kv[3], state = lax.optimization_barrier((kv[3], state))
    last = {3: kv[3]}
    back = []
    for d in (2, 1, 3):
        (coded,) = attend({d: q[d]}, last, prior=state, finish="encode")
        back.append(along(coded, d))
    mine = attend({0: q[0]}, last, prior=state, finish="span", before=q[1])[0]
    parts = local_call(functools.partial(final_kernel, q[0].shape[0]), [((part, WIDTH), BF16)] * 4, (*mine, *back))
    parts = [parts[0]] + [within(parts[j], j) for j in range(1, 4)]
    return local_call(join_kernel, [((part, 4 * WIDTH), BF16)], parts)[0]


def softmax_part(query_rows, per_head_keys, per_head_values, visible, scale):
    scores = (
        jnp.einsum("rhgd,khd->rhgk", query_rows, per_head_keys, preferred_element_type=jnp.float32)
        * scale
    )
    visible_mask = visible[:, None, None, :]
    maxima = jnp.max(jnp.where(visible_mask, scores, NEG_LARGE), axis=-1)
    weights = jnp.where(visible_mask, jnp.exp(scores - maxima[..., None]), 0.0)
    totals = jnp.sum(weights, axis=-1)
    numerators = jnp.einsum(
        "rhgk,khd->rhgd",
        weights.astype(jnp.bfloat16),
        per_head_values,
        preferred_element_type=jnp.float32,
    )
    return (numerators, maxima, totals)


def shards(
    queries, rotated_span_keys, incoming_values, stored_keys, stored_values, shard_lens, span_starts
):
    shard_count = lax.axis_size("kvp")
    device = lax.axis_index("kvp")
    device_local_rows = queries.shape[0]
    cache_slot_count = stored_keys.shape[0]
    query_group_size = QUERY_HEADS // KEY_VALUE_HEADS
    scale = HEAD_SIZE ** (-0.5)
    offsets = jnp.cumsum(shard_lens) - shard_lens
    device_pick = (jnp.arange(shard_count, dtype=jnp.int32) == device).astype(jnp.int32)
    my_start = jnp.sum(offsets * device_pick)
    my_length = jnp.sum(shard_lens * device_pick)
    slot_index = jnp.arange(cache_slot_count, dtype=jnp.int32)
    positions = my_start + slot_index
    live_slots = slot_index < my_length
    per_head_keys = stored_keys.reshape(cache_slot_count, KEY_VALUE_HEADS, HEAD_SIZE)
    per_head_values = stored_values.reshape(cache_slot_count, KEY_VALUE_HEADS, HEAD_SIZE)
    span_index = jnp.arange(SPANS, dtype=jnp.int32)
    every_query = lax.all_gather(queries, "kvp", axis=0, tiled=True)
    overall_rows = every_query.shape[0]
    block_row_range = 64

    def one_block(first):
        rows_here = lax.dynamic_slice_in_dim(every_query, first, block_row_range, 0).reshape(
            block_row_range, KEY_VALUE_HEADS, query_group_size, HEAD_SIZE
        )
        row_ids = first + jnp.arange(block_row_range, dtype=jnp.int32)
        compare = (row_ids // SPAN)[:, None] == span_index[None, :]
        limits = jnp.sum(jnp.where(compare, span_starts[None, :], 0), axis=1)
        visible = live_slots[None, :] & (positions[None, :] < limits[:, None])
        numerators, maxima, totals = softmax_part(
            rows_here, per_head_keys, per_head_values, visible, scale
        )
        return (
            numerators.reshape(block_row_range, QUERY_HEADS * HEAD_SIZE),
            maxima.reshape(block_row_range, QUERY_HEADS),
            totals.reshape(block_row_range, QUERY_HEADS),
        )

    block_starts = jnp.arange(overall_rows // block_row_range, dtype=jnp.int32) * block_row_range
    numerators, maxima, totals = lax.map(one_block, block_starts)
    numerators = numerators.reshape(overall_rows, QUERY_HEADS * HEAD_SIZE)
    maxima = maxima.reshape(overall_rows, QUERY_HEADS)
    totals = totals.reshape(overall_rows, QUERY_HEADS)
    span_key_rows, span_value_rows = (
        lax.all_gather(rotated_span_keys, "kvp", axis=0, tiled=True),
        lax.all_gather(incoming_values, "kvp", axis=0, tiled=True),
    )
    own_ids = device * device_local_rows + jnp.arange(device_local_rows, dtype=jnp.int32)
    key_ids = jnp.arange(overall_rows, dtype=jnp.int32)
    span_visible = (key_ids[None, :] // SPAN == own_ids[:, None] // SPAN) & (
        key_ids[None, :] <= own_ids[:, None]
    )
    local_query = queries.reshape(device_local_rows, KEY_VALUE_HEADS, query_group_size, HEAD_SIZE)
    span_num, span_max, span_total = softmax_part(
        local_query,
        span_key_rows.reshape(overall_rows, KEY_VALUE_HEADS, HEAD_SIZE),
        span_value_rows.reshape(overall_rows, KEY_VALUE_HEADS, HEAD_SIZE),
        span_visible,
        scale,
    )
    span_num = span_num.reshape(device_local_rows, QUERY_HEADS, HEAD_SIZE)
    span_max = span_max.reshape(device_local_rows, QUERY_HEADS)
    span_total = span_total.reshape(device_local_rows, QUERY_HEADS)
    arrived_num, arrived_max, arrived_total = (
        lax.all_to_all(
            numerators.reshape(shard_count, device_local_rows, QUERY_HEADS * HEAD_SIZE),
            "kvp",
            split_axis=0,
            concat_axis=0,
            tiled=True,
        ),
        lax.all_to_all(
            maxima.reshape(shard_count, device_local_rows, QUERY_HEADS),
            "kvp",
            split_axis=0,
            concat_axis=0,
            tiled=True,
        ),
        lax.all_to_all(
            totals.reshape(shard_count, device_local_rows, QUERY_HEADS),
            "kvp",
            split_axis=0,
            concat_axis=0,
            tiled=True,
        ),
    )
    own_max = jnp.max(arrived_max, axis=0)
    factor = jnp.exp(arrived_max - own_max[None])
    summed_num = jnp.sum(
        arrived_num.reshape(shard_count, device_local_rows, QUERY_HEADS, HEAD_SIZE)
        * factor[..., None],
        axis=0,
    )
    summed_total = jnp.sum(arrived_total * factor, axis=0)
    overall = jnp.maximum(own_max, span_max)
    shard_factor = jnp.exp(own_max - overall)
    span_factor = jnp.exp(span_max - overall)
    numerator = summed_num * shard_factor[..., None] + span_num * span_factor[..., None]
    denominator = summed_total * shard_factor + span_total * span_factor
    return (
        (numerator / denominator[..., None])
        .reshape(device_local_rows, QUERY_HEADS * HEAD_SIZE)
        .astype(jnp.bfloat16)
    )


def local(*args):
    queries, keys = args[0], args[3]
    four_by_four = lax.axis_size("kvp") == 16 and queries.shape[0] * 4 * 2 == SPAN and keys.shape[0] % 512 == 0
    if not four_by_four:
        return shards(*args)
    return pipelined(*args)


def solution(mesh):
    in_specs = (
        P(("groups", "kvp"), None),
        P(("groups", "kvp"), None),
        P(("groups", "kvp"), None),
        P(("groups", "kvp"), None),
        P(("groups", "kvp"), None),
        P("groups"),
        P("groups"),
    )
    out_specs = P(("groups", "kvp"), None)
    return jax.shard_map(local, mesh=mesh, in_specs=in_specs, out_specs=out_specs, check_vma=False)
```

```python
import functools

import jax
import jax.numpy as jnp
import numpy as np
from jax import lax
from jax.experimental import pallas as pl
from jax.experimental.pallas import tpu as pltpu
from jax.sharding import PartitionSpec as P

QUERY_HEADS = 32
KEY_VALUE_HEADS = 4
HEAD_SIZE = 128
SPAN = 128
SPANS = 2
GROUP = QUERY_HEADS // KEY_VALUE_HEADS
WIDTH = GROUP * HEAD_SIZE
NEG_LARGE = -1e30
LOG2_SCALE = float(HEAD_SIZE**-0.5 * np.log2(np.e))
CODE = 32767.0
STATS = 4 * GROUP
VMEM_GRANT = 24 * 2**20
F32, BF16, I16 = jnp.float32, jnp.bfloat16, jnp.int16


def row_limit(lens, starts, shard, span, shards, slots):
    start = jnp.int32(0)
    length = jnp.int32(0)
    for j in range(shards):
        n = lens[j]
        start = start + jnp.where(j < shard, n, 0)
        length = jnp.where(j == shard, n, length)
    limit = starts[0]
    for j in range(1, SPANS):
        limit = jnp.where(span == j, starts[j], limit)
    return jnp.clip(jnp.minimum(length, limit - start), 0, slots)


def stack_heads(q):
    return jnp.concatenate([q[:, g * HEAD_SIZE : (g + 1) * HEAD_SIZE] for g in range(GROUP)], axis=0)


def attend(q, k, v, bias):
    s = lax.dot_general(q, k, (((1,), (1,)), ((), ())), preferred_element_type=F32) + bias
    m = jnp.max(s, axis=1, keepdims=True)
    w = jnp.exp2((s - m) * LOG2_SCALE)
    t = jnp.sum(w, axis=1, keepdims=True)
    n = jnp.dot(w.astype(BF16), v, preferred_element_type=F32)
    return n, m, t


def merge(a, b):
    if a is None:
        return b
    m = jnp.maximum(a[1], b[1])
    fa, fb = jnp.exp2((a[1] - m) * LOG2_SCALE), jnp.exp2((b[1] - m) * LOG2_SCALE)
    return a[0] * fa + b[0] * fb, m, a[2] * fa + b[2] * fb


def encode(state, out_ref, rows):
    n, m, t = state
    top = jnp.maximum(jnp.max(jnp.abs(n), axis=1, keepdims=True), 1e-30)
    out_ref[: GROUP * rows, :] = jnp.round(n * (CODE / top)).astype(jnp.int32).astype(I16)
    lane = lax.broadcasted_iota(jnp.int32, (rows, HEAD_SIZE), 1)
    base = jnp.zeros((rows, HEAD_SIZE), F32)
    value = jnp.ones((rows, HEAD_SIZE), F32)
    for g in range(GROUP):
        head = slice(g * rows, (g + 1) * rows)
        base = jnp.where(lane % GROUP == g, m[head], base)
        value = jnp.where(lane % GROUP == g, jnp.where(lane % STATS < 2 * GROUP, top[head], t[head]), value)
    value = jnp.maximum(base * LOG2_SCALE + jnp.log2(value), -2000.0)
    high = jnp.round(value * 16.0)
    low = jnp.round((value - high * (1 / 16.0)) * 524288.0)
    stats = jnp.where(lane % (2 * GROUP) < GROUP, high, low)
    part = rows // 4
    packed = stats[:part]
    for k in range(1, 4):
        packed = jnp.where(lane[:part] // STATS == k, stats[k * part : (k + 1) * part], packed)
    out_ref[GROUP * rows :, :] = packed.astype(jnp.int32).astype(I16)


def columns(j, width):
    return pl.ds(pl.multiple_of(((lax.axis_index("kvp") % 4) ^ j) * width, width), width)


def local_call(kernel, shapes, args, work=0, scratch=(), space=pltpu.VMEM):
    moved = sum(x.size * x.dtype.itemsize for x in args)
    return pl.pallas_call(
        kernel,
        out_shape=[jax.ShapeDtypeStruct(s, t) for s, t in shapes],
        in_specs=[pl.BlockSpec(memory_space=space)] * len(args),
        out_specs=[pl.BlockSpec(memory_space=pltpu.VMEM)] * len(shapes),
        scratch_shapes=scratch,
        compiler_params=pltpu.CompilerParams(vmem_limit_bytes=VMEM_GRANT),
        cost_estimate=pl.CostEstimate(flops=4 * HEAD_SIZE * work, transcendentals=work, bytes_accessed=moved),
    )(*args)


def start_all(pairs, sems):
    copies = [pltpu.make_async_copy(src, dst, sems.at[i]) for i, (src, dst) in enumerate(pairs)]
    for c in copies:
        c.start()
    return copies


def split_far_kernel(q_ref, sk_ref, sv_ref, k_ref, v_ref, *refs):
    (here, core, far, *kv_outs), sems = refs[:5], refs[5]
    rows = here.shape[0]
    pairs = []
    for out, j in zip(kv_outs, (2, 3)):
        pairs.append((k_ref.at[:, columns(j, HEAD_SIZE)], out.at[:, pl.ds(0, HEAD_SIZE)]))
        pairs.append((v_ref.at[:, columns(j, HEAD_SIZE)], out.at[:, pl.ds(HEAD_SIZE, HEAD_SIZE)]))
    for j, out, first in ((2, far, 0), (3, far, rows), (1, core, 0), (0, here, 0)):
        at, to = columns(j, HEAD_SIZE), pl.ds(first, rows)
        pairs.append((q_ref.at[:, columns(j, WIDTH)], out.at[to, pl.ds(0, WIDTH)]))
        pairs.append((sk_ref.at[:, at], out.at[to, pl.ds(WIDTH, HEAD_SIZE)]))
        pairs.append((sv_ref.at[:, at], out.at[to, pl.ds(WIDTH + HEAD_SIZE, HEAD_SIZE)]))
    for c in start_all(pairs, sems):
        c.wait()


def split_near_kernel(shards, lens_ref, starts_ref, k_ref, v_ref, *refs):
    outs, (bias_ref, lens, starts, sems) = refs[:2], refs[2:]
    pairs = [(lens_ref, lens), (starts_ref, starts)]
    for j in (1, 0):
        at = columns(j, HEAD_SIZE)
        pairs.append((k_ref.at[:, at], outs[j].at[:, pl.ds(0, HEAD_SIZE)]))
        pairs.append((v_ref.at[:, at], outs[j].at[:, pl.ds(HEAD_SIZE, HEAD_SIZE)]))
    copies = start_all(pairs, sems)
    me = lax.axis_index("kvp")
    slots = k_ref.shape[0]
    for c in copies[:2]:
        c.wait()
    lane = lax.broadcasted_iota(jnp.int32, (1, slots), 1)
    for span in range(SPANS):
        for j in range(4):
            seen = row_limit(lens, starts, me // 4 * 4 + ((me % 4) ^ j), span, shards, slots)
            bias_ref[span * 4 + j : span * 4 + j + 1, :] = jnp.where(lane < seen, 0.0, NEG_LARGE)
    for c in copies[2:]:
        c.wait()


def stack_kernel(here, core, far, passed, both, only):
    rows = here.shape[0]
    parts = (here[...], core[...], far[:rows, :], passed[rows:, :])
    for j, part in enumerate(parts):
        both[j * rows : (j + 1) * rows, :] = part
        only[j * rows : (j + 1) * rows, :] = part[:, :WIDTH]


def attend_kernel(cfg, bias_ref, *refs):
    _, blocks, pieces, prior, finish, rows = cfg
    refs = list(refs)
    q_refs = [refs.pop(0) for _ in blocks]
    kv = [refs.pop(0) for _ in pieces]
    prior_refs = [(refs.pop(0), refs.pop(0)) for _ in blocks] if prior else None
    span_ref = refs.pop(0) if finish == "span" else None
    outs = refs
    me = lax.axis_index("kvp")
    z, b = me // 4, me % 4
    for i, d in enumerate(blocks):
        q = stack_heads(q_refs[i][:, :WIDTH])
        span = (z ^ d) * rows // SPAN
        state = None
        if prior:
            p_ref, s_ref = prior_refs[i]
            state = (
                jnp.concatenate([p_ref[:, g * HEAD_SIZE : (g + 1) * HEAD_SIZE] for g in range(GROUP)], axis=0),
                s_ref[:, :HEAD_SIZE],
                s_ref[:, HEAD_SIZE:],
            )
        for j, kv_ref in zip(pieces, kv):
            bias = bias_ref[pl.ds(span * 4 + j, 1), :]
            state = merge(state, attend(q, kv_ref[:, :HEAD_SIZE], kv_ref[:, HEAD_SIZE:], bias))
        if finish == "encode":
            encode(state, outs[i], rows)
            continue
        if finish == "span":
            mine, before = q_refs[i], span_ref
            k = jnp.concatenate([mine[:, WIDTH : WIDTH + HEAD_SIZE], before[:, WIDTH : WIDTH + HEAD_SIZE]], axis=0)
            v = jnp.concatenate([mine[:, WIDTH + HEAD_SIZE :], before[:, WIDTH + HEAD_SIZE :]], axis=0)
            s = lax.dot_general(q, k, (((1,), (1,)), ((), ())), preferred_element_type=F32)
            part = rows // 4
            r = lax.broadcasted_iota(jnp.int32, s.shape, 0) % rows
            c = lax.broadcasted_iota(jnp.int32, s.shape, 1)
            r = ((r // part) ^ b) * part + r % part
            here = (((c // part) ^ b) * part + c % part <= r) & (c < rows)
            earlier = (c >= rows) & ((z * rows) % SPAN > 0)
            visible = here | earlier
            s = jnp.where(visible, s, NEG_LARGE)
            m = jnp.max(s, axis=1, keepdims=True)
            w = jnp.where(visible, jnp.exp2((s - m) * LOG2_SCALE), 0.0)
            t = jnp.sum(w, axis=1, keepdims=True)
            state = merge(state, (jnp.dot(w.astype(BF16), v, preferred_element_type=F32), m, t))
        n, m, t = state
        for g in range(GROUP):
            outs[2 * i][:, g * HEAD_SIZE : (g + 1) * HEAD_SIZE] = n[g * rows : (g + 1) * rows]
        outs[2 * i + 1][:, :HEAD_SIZE] = jnp.broadcast_to(m, n.shape)
        outs[2 * i + 1][:, HEAD_SIZE:] = jnp.broadcast_to(t, n.shape)


def attention(bias, shards, q, pieces, prior=None, finish=None, before=None):
    blocks = tuple(q)
    rows = q[blocks[0]].shape[0]
    args = [bias] + [q[d] for d in blocks] + [pieces[j] for j in pieces]
    if prior is not None:
        args += [x for d in blocks for x in prior[d]]
    if finish == "span":
        args.append(before)
    if finish == "encode":
        shapes = [((GROUP * rows + rows // 4, HEAD_SIZE), I16)] * len(blocks)
    else:
        shapes = [((rows, WIDTH), F32), ((GROUP * rows, 2 * HEAD_SIZE), F32)] * len(blocks)
    work = len(blocks) * GROUP * rows * sum(x.shape[0] for x in pieces.values())
    cfg = (shards, blocks, tuple(pieces), prior is not None, finish, rows)
    outs = local_call(functools.partial(attend_kernel, cfg), shapes, args, work=work)
    if finish == "encode":
        return outs
    return {d: (outs[2 * i], outs[2 * i + 1]) for i, d in enumerate(blocks)}


def final_kernel(rows, n_ref, s_ref, *refs):
    codes, outs = refs[:3], refs[3:]
    part = rows // 4
    lane = lax.broadcasted_iota(jnp.int32, (rows, HEAD_SIZE), 1)
    m = jnp.zeros((rows, HEAD_SIZE), F32)
    t = jnp.zeros((rows, HEAD_SIZE), F32)
    for g in range(GROUP):
        head = slice(g * rows, (g + 1) * rows)
        m = jnp.where(lane == g, s_ref[head, :HEAD_SIZE], m)
        t = jnp.where(lane == g, s_ref[head, HEAD_SIZE:], t)
    m = m * LOG2_SCALE
    tops, sums = [], []
    for c in codes:
        x = c[GROUP * rows :, :].astype(F32)
        x = jnp.concatenate([x] + [pltpu.roll(x, 4 * STATS - k * STATS, 1) for k in range(1, 4)], axis=0)
        x = x * (1 / 16.0) + pltpu.roll(x, HEAD_SIZE - GROUP, 1) * (1 / 524288.0)
        tops.append(x)
        sums.append(pltpu.roll(x, HEAD_SIZE - 2 * GROUP, 1))
    over = m
    for x in sums:
        over = jnp.maximum(over, x)
    mine = jnp.exp2(m - over)
    total = t * mine
    for x in sums:
        total = total + jnp.exp2(x - over)
    inverse = 1.0 / jnp.where(lane < GROUP, total, 1.0)
    factors = [mine * inverse] + [jnp.exp2(jnp.where(lane < GROUP, x - over, 0.0)) * (inverse * (1 / CODE)) for x in tops]
    for g in range(GROUP):
        cols = slice(g * HEAD_SIZE, (g + 1) * HEAD_SIZE)
        n = n_ref[:, cols] * factors[0][:, g : g + 1]
        for c, f in zip(codes, factors[1:]):
            n = n + c[g * rows : (g + 1) * rows, :].astype(F32) * f[:, g : g + 1]
        n = n.astype(BF16)
        for k in range(4):
            outs[k][:, cols] = n[k * part : (k + 1) * part]


def join_kernel(*refs):
    for j in range(4):
        refs[4][:, columns(j, WIDTH)] = refs[j][...]


def pipelined(queries, span_keys, span_values, keys, values, shard_lens, span_starts):
    n = lax.axis_size("kvp")
    zs = n // 4
    tables = (shard_lens, span_starts)

    def within(x, j):
        return lax.ppermute(x, "kvp", [(i, i ^ j) for i in range(n)])

    def along(x, d):
        return lax.ppermute(x, "kvp", [(i, i ^ (4 * d)) for i in range(n)])

    def attend(*args, **kwargs):
        return attention(bias, n, *args, **kwargs)

    part, slots = queries.shape[0], keys.shape[0]
    wide = WIDTH + 2 * HEAD_SIZE
    ins = [queries, span_keys, span_values, keys, values]
    ins, tables = ([pltpu.with_memory_space_constraint(x, pltpu.HBM) for x in xs] for xs in (ins, tables))
    here, core, far, kv2, kv3 = local_call(
        split_far_kernel,
        [((part, wide), BF16)] * 2 + [((2 * part, wide), BF16)] + [((slots, 2 * HEAD_SIZE), BF16)] * 2,
        ins,
        scratch=[pltpu.SemaphoreType.DMA((16,))],
        space=pltpu.HBM,
    )
    kv0, kv1, bias = local_call(
        functools.partial(split_near_kernel, n),
        [((slots, 2 * HEAD_SIZE), BF16)] * 2 + [((SPANS * 4, slots), F32)],
        tables + ins[3:],
        scratch=[pltpu.SMEM(x.shape, x.dtype) for x in tables] + [pltpu.SemaphoreType.DMA((6,))],
        space=pltpu.HBM,
    )
    core, far = within(core, 1), within(far, 2)
    q_parts = (here, core, far, within(far, 1))
    kv = {0: kv0, 1: within(kv1, 1), 2: within(kv2, 2), 3: within(kv3, 3)}
    stacked, only = local_call(stack_kernel, [((4 * part, wide), BF16), ((4 * part, WIDTH), BF16)], q_parts)
    q = {0: stacked, 1: along(stacked, 1)} | {d: along(only, d) for d in range(2, zs)}

    near = {j: kv[j] for j in (0, 1)}
    state = attend({0: q[0]}, near)
    near[2] = kv[2]
    state |= attend({1: q[1]}, near)
    state |= attend({2: q[2]}, near)
    state |= attend({3: q[3]}, near)
    kv[3], state = lax.optimization_barrier((kv[3], state))
    last = {3: kv[3]}
    both = {2: kv[2], 3: kv[3]}
    back = []
    for d in (2, 1, 3):
        (coded,) = attend({d: q[d]}, last, prior=state, finish="encode")
        back.append(along(coded, d))
    mine = attend({0: q[0]}, both, prior=state, finish="span", before=q[1])[0]
    parts = local_call(functools.partial(final_kernel, q[0].shape[0]), [((part, WIDTH), BF16)] * 4, (*mine, *back))
    parts = [parts[0]] + [within(parts[j], j) for j in range(1, 4)]
    return local_call(join_kernel, [((part, 4 * WIDTH), BF16)], parts)[0]


def softmax_part(query_rows, per_head_keys, per_head_values, visible, scale):
    scores = (
        jnp.einsum("rhgd,khd->rhgk", query_rows, per_head_keys, preferred_element_type=jnp.float32)
        * scale
    )
    visible_mask = visible[:, None, None, :]
    maxima = jnp.max(jnp.where(visible_mask, scores, NEG_LARGE), axis=-1)
    weights = jnp.where(visible_mask, jnp.exp(scores - maxima[..., None]), 0.0)
    totals = jnp.sum(weights, axis=-1)
    numerators = jnp.einsum(
        "rhgk,khd->rhgd",
        weights.astype(jnp.bfloat16),
        per_head_values,
        preferred_element_type=jnp.float32,
    )
    return (numerators, maxima, totals)


def shards(
    queries, rotated_span_keys, incoming_values, stored_keys, stored_values, shard_lens, span_starts
):
    shard_count = lax.axis_size("kvp")
    device = lax.axis_index("kvp")
    device_local_rows = queries.shape[0]
    cache_slot_count = stored_keys.shape[0]
    query_group_size = QUERY_HEADS // KEY_VALUE_HEADS
    scale = HEAD_SIZE ** (-0.5)
    offsets = jnp.cumsum(shard_lens) - shard_lens
    device_pick = (jnp.arange(shard_count, dtype=jnp.int32) == device).astype(jnp.int32)
    my_start = jnp.sum(offsets * device_pick)
    my_length = jnp.sum(shard_lens * device_pick)
    slot_index = jnp.arange(cache_slot_count, dtype=jnp.int32)
    positions = my_start + slot_index
    live_slots = slot_index < my_length
    per_head_keys = stored_keys.reshape(cache_slot_count, KEY_VALUE_HEADS, HEAD_SIZE)
    per_head_values = stored_values.reshape(cache_slot_count, KEY_VALUE_HEADS, HEAD_SIZE)
    span_index = jnp.arange(SPANS, dtype=jnp.int32)
    every_query = lax.all_gather(queries, "kvp", axis=0, tiled=True)
    overall_rows = every_query.shape[0]
    block_row_range = 64

    def one_block(first):
        rows_here = lax.dynamic_slice_in_dim(every_query, first, block_row_range, 0).reshape(
            block_row_range, KEY_VALUE_HEADS, query_group_size, HEAD_SIZE
        )
        row_ids = first + jnp.arange(block_row_range, dtype=jnp.int32)
        compare = (row_ids // SPAN)[:, None] == span_index[None, :]
        limits = jnp.sum(jnp.where(compare, span_starts[None, :], 0), axis=1)
        visible = live_slots[None, :] & (positions[None, :] < limits[:, None])
        numerators, maxima, totals = softmax_part(
            rows_here, per_head_keys, per_head_values, visible, scale
        )
        return (
            numerators.reshape(block_row_range, QUERY_HEADS * HEAD_SIZE),
            maxima.reshape(block_row_range, QUERY_HEADS),
            totals.reshape(block_row_range, QUERY_HEADS),
        )

    block_starts = jnp.arange(overall_rows // block_row_range, dtype=jnp.int32) * block_row_range
    numerators, maxima, totals = lax.map(one_block, block_starts)
    numerators = numerators.reshape(overall_rows, QUERY_HEADS * HEAD_SIZE)
    maxima = maxima.reshape(overall_rows, QUERY_HEADS)
    totals = totals.reshape(overall_rows, QUERY_HEADS)
    span_key_rows, span_value_rows = (
        lax.all_gather(rotated_span_keys, "kvp", axis=0, tiled=True),
        lax.all_gather(incoming_values, "kvp", axis=0, tiled=True),
    )
    own_ids = device * device_local_rows + jnp.arange(device_local_rows, dtype=jnp.int32)
    key_ids = jnp.arange(overall_rows, dtype=jnp.int32)
    span_visible = (key_ids[None, :] // SPAN == own_ids[:, None] // SPAN) & (
        key_ids[None, :] <= own_ids[:, None]
    )
    local_query = queries.reshape(device_local_rows, KEY_VALUE_HEADS, query_group_size, HEAD_SIZE)
    span_num, span_max, span_total = softmax_part(
        local_query,
        span_key_rows.reshape(overall_rows, KEY_VALUE_HEADS, HEAD_SIZE),
        span_value_rows.reshape(overall_rows, KEY_VALUE_HEADS, HEAD_SIZE),
        span_visible,
        scale,
    )
    span_num = span_num.reshape(device_local_rows, QUERY_HEADS, HEAD_SIZE)
    span_max = span_max.reshape(device_local_rows, QUERY_HEADS)
    span_total = span_total.reshape(device_local_rows, QUERY_HEADS)
    arrived_num, arrived_max, arrived_total = (
        lax.all_to_all(
            numerators.reshape(shard_count, device_local_rows, QUERY_HEADS * HEAD_SIZE),
            "kvp",
            split_axis=0,
            concat_axis=0,
            tiled=True,
        ),
        lax.all_to_all(
            maxima.reshape(shard_count, device_local_rows, QUERY_HEADS),
            "kvp",
            split_axis=0,
            concat_axis=0,
            tiled=True,
        ),
        lax.all_to_all(
            totals.reshape(shard_count, device_local_rows, QUERY_HEADS),
            "kvp",
            split_axis=0,
            concat_axis=0,
            tiled=True,
        ),
    )
    own_max = jnp.max(arrived_max, axis=0)
    factor = jnp.exp(arrived_max - own_max[None])
    summed_num = jnp.sum(
        arrived_num.reshape(shard_count, device_local_rows, QUERY_HEADS, HEAD_SIZE)
        * factor[..., None],
        axis=0,
    )
    summed_total = jnp.sum(arrived_total * factor, axis=0)
    overall = jnp.maximum(own_max, span_max)
    shard_factor = jnp.exp(own_max - overall)
    span_factor = jnp.exp(span_max - overall)
    numerator = summed_num * shard_factor[..., None] + span_num * span_factor[..., None]
    denominator = summed_total * shard_factor + span_total * span_factor
    return (
        (numerator / denominator[..., None])
        .reshape(device_local_rows, QUERY_HEADS * HEAD_SIZE)
        .astype(jnp.bfloat16)
    )


def local(*args):
    queries, keys = args[0], args[3]
    four_by_four = lax.axis_size("kvp") == 16 and queries.shape[0] * 4 * 2 == SPAN and keys.shape[0] % 512 == 0
    if not four_by_four:
        return shards(*args)
    return pipelined(*args)


def solution(mesh):
    in_specs = (
        P(("groups", "kvp"), None),
        P(("groups", "kvp"), None),
        P(("groups", "kvp"), None),
        P(("groups", "kvp"), None),
        P(("groups", "kvp"), None),
        P("groups"),
        P("groups"),
    )
    out_specs = P(("groups", "kvp"), None)
    return jax.shard_map(local, mesh=mesh, in_specs=in_specs, out_specs=out_specs, check_vma=False)
```
